256 devices in a mesh: gx: 32 (over y_hi, z, core), gy: 4 (over x), gz: 2 (over y_lo).
Axes of the slice: x: 4, y: 4 (y_hi: 2, y_lo: 2; y = y_hi * 2 + y_lo), z: 8, core: 2. Of those that a mesh axis runs over, the one named last changes fastest.
Arguments:
- elevation: float32 [2048, 8192], P('gx', ('gy', 'gz')), may hold values from -1 to 1
- surface_potential: float32 [2048, 8192], P('gx', ('gy', 'gz')), may hold values from -2 to 2
- seabed: int32 [2048, 8192], P('gx', 'gy'), may hold values from 384 to 1023
- interior_potential: float32 [16, 2048, 8192], P('gz', 'gx', 'gy'), may hold values from -1.5 to 1.5
Outputs:
- new_elevation: float32 [2048, 8192], P('gx', ('gy', 'gz'))
- new_potential: float32 [2048, 8192], P('gx', ('gy', 'gz'))
- laplace_apply: float32 [16, 2048, 8192], P('gz', 'gx', 'gy')
The draws below stay inside these ranges and needn't reach their ends.
All inputs are finite; a program needn't handle non-finite values.
Results may differ from the reference program's by a relative error of at most 0.0003.
Values sent between devices are 32-bit elements; how exact they have to be, the bound alone decides.
A program may use at most 64 MiB of HBM per device.

```python
import jax
import jax.numpy as jnp
from jax import lax

NX = 2048
NY = 8192
NL = 16


def plant(array, own_key, smallest, largest):
    extent = array.shape
    place = [jax.random.randint(jax.random.fold_in(own_key, axis), (), 0, extent[axis]) for axis in range(len(extent))]
    array = array.at[tuple(place)].set(smallest)
    longest = extent.index(max(extent))
    place[longest] = (place[longest] + 1) % extent[longest]
    return array.at[tuple(place)].set(largest)


def level_of(key, extent, split, smallest, top_value):
    def one(dim, shards_of):
        draws = jax.random.uniform(jax.random.fold_in(jax.random.fold_in(key, 6), dim), (shards_of,), jnp.float32, smallest / len(split), top_value / len(split))
        return jnp.repeat(jnp.exp(draws), extent[dim] // shards_of).reshape((-1,) + (1,) * (len(extent) - dim - 1))

    level = one(*split[0])
    for cut in split[1:]:
        level = level * one(*cut)
    return level


def scatter_about(rng, dims, spread, limit, shards=(), kind=jnp.bfloat16):
    result = jax.random.normal(rng, dims, jnp.float32) * spread
    if len(shards) > 0:
        result = level_of(rng, dims, shards, -0.22, 0.18) * result
    return jnp.clip(result, min=-limit, max=limit).astype(kind)


def setup_inputs(seed: int = 0) -> dict:
    seeds = jax.random.split(jax.random.key(seed), 5)
    return {
        "elevation": scatter_about(seeds[0], (NX, NY), 0.25, 1.0, ((0, 32), (1, 8)), jnp.float32),
        "surface_potential": scatter_about(seeds[1], (NX, NY), 0.5, 2.0, ((0, 32), (1, 8)), jnp.float32),
        "seabed": plant(jax.random.randint(seeds[2], (NX, NY), 384, 1024), jax.random.fold_in(seeds[2], 1), 384, 1023).astype(jnp.int32),
        "interior_potential": scatter_about(seeds[3], (NL, NX, NY), 0.25, 1.5, ((0, 2), (1, 32), (2, 4)), jnp.float32),
    }


time_step = 0.05
depth_unit = 0.015625


def shifted(source, step_north, step_east):
    return jnp.roll(source, (-step_north, -step_east), axis=(0, 1))


def first_north(source):
    return (8.0 * (shifted(source, 1, 0) - shifted(source, -1, 0)) - (shifted(source, 2, 0) - shifted(source, -2, 0))) / 12.0


def first_east(source):
    return (8.0 * (shifted(source, 0, 1) - shifted(source, 0, -1)) - (shifted(source, 0, 2) - shifted(source, 0, -2))) / 12.0


def curvature(source):
    north = (-shifted(source, 2, 0) + 16.0 * shifted(source, 1, 0) - 30.0 * source + 16.0 * shifted(source, -1, 0) - shifted(source, -2, 0)) / 12.0
    east = (-shifted(source, 0, 2) + 16.0 * shifted(source, 0, 1) - 30.0 * source + 16.0 * shifted(source, 0, -1) - shifted(source, 0, -2)) / 12.0
    return north + east


def rates(height, poten):
    height_north = first_north(height)
    height_east = first_east(height)
    poten_north = first_north(poten)
    poten_east = first_east(poten)
    rate_height = curvature(poten) - (height_north * poten_north + height_east * poten_east)
    rate_potential = -height - 0.5 * (poten_north * poten_north + poten_east * poten_east)
    return rate_height, rate_potential


def centred_north(source):
    return 0.5 * (shifted(source, 1, 0) - shifted(source, -1, 0))


def centred_east(source):
    return 0.5 * (shifted(source, 0, 1) - shifted(source, 0, -1))


def reference(elevation, surface_potential, seabed, interior_potential):
    rate_first, rate_second = rates(elevation, surface_potential)
    elevation_one = elevation + time_step * rate_first
    potential_one = surface_potential + time_step * rate_second
    rate_third, rate_fourth = rates(elevation_one, potential_one)
    new_elevation = 0.5 * (elevation + elevation_one + time_step * rate_third)
    new_potential = 0.5 * (surface_potential + potential_one + time_step * rate_fourth)
    depth = seabed.astype(jnp.float32) * depth_unit
    column = depth + new_elevation
    depth_north = centred_north(depth)
    depth_east = centred_east(depth)
    column_north = centred_north(column)
    column_east = centred_east(column)
    spacing = 1.0 / NL

    def one_layer(layer_index):
        centre = lax.dynamic_index_in_dim(interior_potential, layer_index, 0, keepdims=False)
        ghost_below = lax.dynamic_index_in_dim(interior_potential, jnp.maximum(layer_index - 1, 0).astype(jnp.int32), 0, keepdims=False)
        inner_above = lax.dynamic_index_in_dim(interior_potential, jnp.minimum(layer_index + 1, NL - 1).astype(jnp.int32), 0, keepdims=False)
        ghost_above = jnp.where(layer_index == NL - 1, 2.0 * new_potential - centre, inner_above)
        sigma_level = (layer_index.astype(jnp.float32) + 0.5) / NL
        slope_north = (depth_north - sigma_level * column_north) / column
        slope_east = (depth_east - sigma_level * column_east) / column
        second_north = shifted(centre, 1, 0) - 2.0 * centre + shifted(centre, -1, 0)
        second_east = shifted(centre, 0, 1) - 2.0 * centre + shifted(centre, 0, -1)
        mixed_north = (centred_north(ghost_above) - centred_north(ghost_below)) / (2.0 * spacing)
        mixed_east = (centred_east(ghost_above) - centred_east(ghost_below)) / (2.0 * spacing)
        vertical = (ghost_above - 2.0 * centre + ghost_below) / (spacing * spacing)
        weight = slope_north * slope_north + slope_east * slope_east + 1.0 / (column * column)
        return second_north + second_east + 2.0 * slope_north * mixed_north + 2.0 * slope_east * mixed_east + weight * vertical

    laplace_apply = lax.map(one_layer, jnp.arange(NL, dtype=jnp.int32))
    return new_elevation, new_potential, laplace_apply
```

```python
import jax
import jax.numpy as jnp
from jax import lax
from jax.experimental import pallas as pl
from jax.experimental.pallas import tpu as pltpu
from jax.sharding import PartitionSpec as P

MESH = pl.DeviceIdType.MESH
TIME_STEP = 0.05
DEPTH_UNIT = 0.015625

ROWS = 64
HALF = 1024
WIDE = 2048
LAYERS = 8
STRIP = 256


def lane_shift(x, by):
    return pltpu.roll(x, (-by) % x.shape[-1], axis=len(x.shape) - 1)


def row_shift(before, here, after, by):
    rows = lax.broadcasted_iota(jnp.int32, here.shape, 0)
    moved = pltpu.roll(here, (-by) % 8, axis=0)
    if by > 0:
        return jnp.where(rows >= 8 - by, pltpu.roll(after, 8 - by, axis=0), moved)
    return jnp.where(rows < -by, pltpu.roll(before, -by, axis=0), moved)


def section(height, poten):
    def parts(tiles):
        before, here, after = tiles
        north = [row_shift(before, here, after, by) for by in (-2, -1, 1, 2)]
        east = [lane_shift(here, by) for by in (-2, -1, 1, 2)]
        return north, east

    def first(m2, m1, p1, p2):
        return 8.0 * (p1 - m1) - (p2 - m2)

    height_north, height_east = parts(height)
    poten_north, poten_east = parts(poten)
    e_n, e_e = first(*height_north), first(*height_east)
    p_n, p_e = first(*poten_north), first(*poten_east)
    near = (poten_north[1] + poten_north[2]) + (poten_east[1] + poten_east[2])
    far = (poten_north[0] + poten_north[3]) + (poten_east[0] + poten_east[3])
    curve = 16.0 * near - far - 60.0 * poten[1]
    rate_height = curve * (1.0 / 12.0) - (e_n * p_n + e_e * p_e) * (1.0 / 144.0)
    rate_poten = -height[1] - (p_n * p_n + p_e * p_e) * (0.5 / 144.0)
    return rate_height, rate_poten


def kernel(
    e_hbm, p_hbm, seabed_hbm, vol_hbm,
    new_e_out, new_p_out, lap_ref,
    raw, one, new, seabed, vol, depth, column,
    local_sem, send_sem, recv_sem,
):
    gx, gy, gz = lax.axis_index("gx"), lax.axis_index("gy"), lax.axis_index("gz")
    block = 2 * gy + gz

    def device(dx, db):
        at = lax.rem(block + db + 8, 8)
        return (lax.rem(gx + dx + 32, 32), lax.div(at, 2), lax.rem(at, 2))

    side = 1 - 2 * gz
    partner = (gx, gy, 1 - gz)
    ghost = 9 * gz
    edge = 7 * (1 - gz)
    own = pl.multiple_of(128 + HALF * gz, 128)
    outer = pl.multiple_of((WIDE + 128) * gz, 128)

    mid = pl.ds(8, ROWS)
    loads = [
        pltpu.make_async_copy(e_hbm, raw.at[0, mid, pl.ds(128, HALF)], local_sem.at[0]),
        pltpu.make_async_copy(p_hbm, raw.at[1, mid, pl.ds(128, HALF)], local_sem.at[1]),
        pltpu.make_async_copy(seabed_hbm, seabed.at[mid, pl.ds(128, WIDE)], local_sem.at[2]),
        pltpu.make_async_copy(
            vol_hbm, vol.at[pl.ds(1, LAYERS), mid, pl.ds(128, WIDE)], local_sem.at[3]
        ),
    ]
    for load in loads:
        load.start()

    near = [(dx, db) for dx in (-1, 0, 1) for db in (-1, 0, 1) if (dx, db) != (0, 0)]
    barrier = pltpu.get_barrier_semaphore()
    for dx, db in near + [(0, -2), (0, 2)]:
        pl.semaphore_signal(barrier, inc=1, device_id=device(dx, db), device_id_type=MESH)
    pl.semaphore_signal(barrier, inc=1, device_id=device(0, 3 * side), device_id_type=MESH)
    pl.semaphore_wait(barrier, 11)

    copies = []

    def send(src, dst, to):
        at = len(copies)
        copy = pltpu.make_async_remote_copy(
            src, dst, send_sem.at[at], recv_sem.at[at], device_id=to, device_id_type=MESH
        )
        copy.start()
        copies.append(copy)

    loads[0].wait()
    loads[1].wait()
    row_src = {1: pl.ds(64, 8), -1: pl.ds(8, 8), 0: mid}
    row_dst = {1: pl.ds(0, 8), -1: pl.ds(72, 8), 0: mid}
    lane_src = {1: pl.ds(HALF, 128), -1: pl.ds(128, 128), 0: pl.ds(128, HALF)}
    lane_dst = {1: pl.ds(0, 128), -1: pl.ds(HALF + 128, 128), 0: pl.ds(128, HALF)}
    for dx, db in near:
        send(
            raw.at[:, row_src[dx], lane_src[db]],
            raw.at[:, row_dst[dx], lane_dst[db]],
            device(dx, db),
        )
    raw_copies = list(copies)

    send(vol_hbm.at[edge], vol.at[ghost, mid, pl.ds(128, WIDE)], partner)
    for by, src, dst in ((1, pl.ds(56, 8), pl.ds(0, 8)), (-1, pl.ds(0, 8), pl.ds(72, 8))):
        to = device(by, 0)
        across = device(by, side)
        send(seabed_hbm.at[src], seabed.at[dst, pl.ds(128, WIDE)], to)
        send(
            vol_hbm.at[:, src], vol.at[pl.ds(1, LAYERS), dst, pl.ds(128, WIDE)], to
        )
        send(vol_hbm.at[edge, src], vol.at[ghost, dst, pl.ds(128, WIDE)], across)
    for by, src, dst in (
        (1, pl.ds(WIDE - 128, 128), pl.ds(0, 128)),
        (-1, pl.ds(0, 128), pl.ds(WIDE + 128, 128)),
    ):
        to = device(0, 2 * by)
        across = (gx, lax.rem(gy + by + 4, 4), 1 - gz)
        send(seabed_hbm.at[:, src], seabed.at[mid, dst], to)
        send(vol_hbm.at[:, :, src], vol.at[pl.ds(1, LAYERS), mid, dst], to)
        send(vol_hbm.at[edge, :, src], vol.at[ghost, mid, dst], across)

    for copy in raw_copies:
        copy.wait_recv()

    def tiles(ref, field, r):
        def rows(i):
            return ref[field, pl.ds(pl.multiple_of(8 * i, 8), 8), :]

        return rows(jnp.maximum(r - 1, 0)), rows(r), rows(jnp.minimum(r + 1, 9))

    @pl.loop(0, 10)
    def _(r):
        height, poten = tiles(raw, 0, r), tiles(raw, 1, r)
        rate_height, rate_poten = section(height, poten)
        at = pl.ds(pl.multiple_of(8 * r, 8), 8)
        one[0, at, :] = height[1] + TIME_STEP * rate_height
        one[1, at, :] = poten[1] + TIME_STEP * rate_poten

    @pl.loop(0, 10)
    def _(r):
        height, poten = tiles(one, 0, r), tiles(one, 1, r)
        rates = section(height, poten)
        at = pl.ds(pl.multiple_of(8 * r, 8), 8)
        for f in (0, 1):
            first = (height, poten)[f][1]
            value = 0.5 * (raw[f, at, :] + first + TIME_STEP * rates[f])
            new[f, at, pl.ds(own, HALF)] = value[:, 128 : 128 + HALF]
            new[f, at, pl.ds(outer, 128)] = jnp.where(
                gz == 0, value[:, :128], value[:, HALF + 128 :]
            )

    outs = [
        pltpu.make_async_copy(new.at[0, mid, pl.ds(own, HALF)], new_e_out, local_sem.at[4]),
        pltpu.make_async_copy(new.at[1, mid, pl.ds(own, HALF)], new_p_out, local_sem.at[5]),
    ]
    for out in outs:
        out.start()
    send(new.at[:, :, pl.ds(own, HALF)], new.at[:, :, pl.ds(own, HALF)], partner)
    send(new.at[:, :, pl.ds(outer, 128)], new.at[:, :, pl.ds(outer, 128)], partner)

    for load in loads[2:]:
        load.wait()
    for copy in copies[len(raw_copies) :]:
        copy.wait_recv()

    @pl.loop(0, 10)
    def _(r):
        at = pl.ds(pl.multiple_of(8 * r, 8), 8)
        bed = seabed[at, :].astype(jnp.float32) * DEPTH_UNIT
        depth[at, :] = bed
        column[at, :] = bed + new[0, at, :]

        @pl.when(gz == 0)
        def _():
            vol[0, at, :] = vol[1, at, :]

        @pl.when(gz == 1)
        def _():
            vol[9, at, :] = 2.0 * new[1, at, :] - vol[8, at, :]

    first_sigma = (8.0 * gz.astype(jnp.float32) + 0.5) * 0.0625

    def differences(load):
        def parts(lanes, back):
            return load(lanes, back)

        centre = load(0, STRIP)
        wide = load(-128, STRIP + 256)
        return centre, wide

    @pl.loop(0, 8)
    def _(r):
        row = pl.multiple_of(8 * r + 8, 8)

        @pl.loop(0, WIDE // STRIP)
        def _(s):
            lane = pl.multiple_of(s * STRIP, 128)

            def around(ref, layer):
                def rows(at, lanes):
                    at = pl.ds(at, 8)
                    return ref[at, lanes] if layer is None else ref[layer, at, lanes]

                inner = pl.ds(lane + 128, STRIP)
                wide = rows(row, pl.ds(lane, STRIP + 256))
                here = wide[:, 128 : 128 + STRIP]
                before, after = rows(row - 8, inner), rows(row + 8, inner)
                up, down = row_shift(before, here, after, 1), row_shift(before, here, after, -1)
                right = lane_shift(wide, 1)[:, 128 : 128 + STRIP]
                left = lane_shift(wide, -1)[:, 128 : 128 + STRIP]
                return here, up - down, right - left, (up + down) + (right + left)

            here, column_north, column_east, _ = around(column, None)
            _, depth_north, depth_east, _ = around(depth, None)
            inverse = 1.0 / here
            scale = 4.0 * inverse
            step_north = column_north * scale
            step_east = column_east * scale
            slope_north = depth_north * scale - first_sigma * step_north
            slope_east = depth_east * scale - first_sigma * step_east
            step_north = step_north * 0.0625
            step_east = step_east * 0.0625
            base = 64.0 * inverse * inverse
            below = around(vol, 0)
            middle = around(vol, 1)
            for k in range(LAYERS):
                above = around(vol, k + 2)
                weight = slope_north * slope_north + slope_east * slope_east + base
                four = 4.0 * middle[0]
                vertical = 4.0 * (above[0] + below[0]) - 2.0 * four
                lap_ref[k, pl.ds(row - 8, 8), pl.ds(lane, STRIP)] = (
                    (middle[3] - four)
                    + slope_north * (above[1] - below[1])
                    + slope_east * (above[2] - below[2])
                    + weight * vertical
                )
                slope_north = slope_north - step_north
                slope_east = slope_east - step_east
                below, middle = middle, above

    for out in outs:
        out.wait()
    for copy in copies:
        copy.wait_send()


def shards(elevation, surface_potential, seabed, interior_potential):
    copies = 8 + 1 + 6 + 6 + 2
    hbm = pl.BlockSpec(memory_space=pltpu.HBM)
    f32 = jnp.float32
    return pl.pallas_call(
        kernel,
        out_shape=(
            jax.ShapeDtypeStruct((ROWS, HALF), f32),
            jax.ShapeDtypeStruct((ROWS, HALF), f32),
            pltpu.VMEM((LAYERS, ROWS, WIDE), f32),
        ),
        in_specs=[hbm] * 4,
        out_specs=(hbm, hbm, pl.BlockSpec(memory_space=pltpu.VMEM)),
        scratch_shapes=[
            pltpu.VMEM((2, ROWS + 16, HALF + 256), f32),
            pltpu.VMEM((2, ROWS + 16, HALF + 256), f32),
            pltpu.VMEM((2, ROWS + 16, WIDE + 256), f32),
            pltpu.VMEM((ROWS + 16, WIDE + 256), jnp.int32),
            pltpu.VMEM((LAYERS + 2, ROWS + 16, WIDE + 256), f32),
            pltpu.VMEM((ROWS + 16, WIDE + 256), f32),
            pltpu.VMEM((ROWS + 16, WIDE + 256), f32),
            pltpu.SemaphoreType.DMA((6,)),
            pltpu.SemaphoreType.DMA((copies,)),
            pltpu.SemaphoreType.DMA((copies,)),
        ],
        compiler_params=pltpu.CompilerParams(
            collective_id=0, has_side_effects=True, vmem_limit_bytes=40 << 20
        ),
        name="wave_step",
    )(elevation, surface_potential, seabed, interior_potential)


def solution(mesh):
    return jax.shard_map(
        shards,
        mesh=mesh,
        in_specs=(P("gx", ("gy", "gz")), P("gx", ("gy", "gz")), P("gx", "gy"), P("gz", "gx", "gy")),
        out_specs=(P("gx", ("gy", "gz")), P("gx", ("gy", "gz")), P("gz", "gx", "gy")),
        check_vma=False,
    )
```

```python
import jax
import jax.numpy as jnp
from jax import lax
from jax.experimental import pallas as pl
from jax.experimental.pallas import tpu as pltpu
from jax.sharding import PartitionSpec as P

MESH = pl.DeviceIdType.MESH
TIME_STEP = 0.05
DEPTH_UNIT = 0.015625

ROWS = 64
HALF = 1024
WIDE = 2048
LAYERS = 8
STRIP = 512
EARLY = 40
COPIES = 32


def lane_shift(x, by):
    return pltpu.roll(x, (-by) % x.shape[-1], axis=len(x.shape) - 1)


def row_shift(before, here, after, by):
    rows = lax.broadcasted_iota(jnp.int32, here.shape, 0)
    moved = pltpu.roll(here, (-by) % 8, axis=0)
    if by > 0:
        return jnp.where(rows >= 8 - by, pltpu.roll(after, 8 - by, axis=0), moved)
    return jnp.where(rows < -by, pltpu.roll(before, -by, axis=0), moved)


def section(height, poten):
    def parts(tiles):
        before, here, after = tiles
        north = [row_shift(before, here, after, by) for by in (-2, -1, 1, 2)]
        east = [lane_shift(here, by) for by in (-2, -1, 1, 2)]
        return north, east

    def first(m2, m1, p1, p2):
        return 8.0 * (p1 - m1) - (p2 - m2)

    height_north, height_east = parts(height)
    poten_north, poten_east = parts(poten)
    e_n, e_e = first(*height_north), first(*height_east)
    p_n, p_e = first(*poten_north), first(*poten_east)
    near = (poten_north[1] + poten_north[2]) + (poten_east[1] + poten_east[2])
    far = (poten_north[0] + poten_north[3]) + (poten_east[0] + poten_east[3])
    curve = 16.0 * near - far - 60.0 * poten[1]
    rate_height = curve * (1.0 / 12.0) - (e_n * p_n + e_e * p_e) * (1.0 / 144.0)
    rate_poten = -height[1] - (p_n * p_n + p_e * p_e) * (0.5 / 144.0)
    return rate_height, rate_poten


def kernel(
    e_hbm, p_hbm, seabed_hbm, vol_hbm,
    new_e_out, new_p_out, lap_ref,
    raw, one, new, seabed, vol, depth, column,
    side_x, side_send, side_recv, side_in,
    rows_out, rows_in, ring_rows, new_rows_out, new_rows_in, cols_out, cols_in,
    local_sem, send_sem, recv_sem,
):
    gx, gy, gz = lax.axis_index("gx"), lax.axis_index("gy"), lax.axis_index("gz")
    block = 2 * gy + gz

    def device(dx, db):
        at = lax.rem(block + db + 8, 8)
        return (lax.rem(gx + dx + 32, 32), lax.div(at, 2), lax.rem(at, 2))

    side = 1 - 2 * gz
    partner = (gx, gy, 1 - gz)
    theirs = 9 * gz
    mine = 9 - theirs
    edge = 7 * (1 - gz)
    mid = pl.ds(8, ROWS)
    inner = pl.ds(128, HALF)
    tile = pl.ds(128, WIDE)

    loads = [
        pltpu.make_async_copy(e_hbm, raw.at[0, mid, inner], local_sem.at[0]),
        pltpu.make_async_copy(p_hbm, raw.at[1, mid, inner], local_sem.at[1]),
        pltpu.make_async_copy(seabed_hbm, seabed.at[:, tile], local_sem.at[2]),
        pltpu.make_async_copy(vol_hbm, vol.at[pl.ds(1, LAYERS), mid, tile], local_sem.at[3]),
    ]
    for load in loads:
        load.start()

    barrier = pltpu.get_barrier_semaphore()
    corners = [(-1, -1), (-1, 1), (1, -1), (1, 1)]
    for dx, db in corners + [(-1, 0), (1, 0), (0, -1), (0, 1), (0, -2), (0, 2)]:
        pl.semaphore_signal(barrier, inc=1, device_id=device(dx, db), device_id_type=MESH)

    lanes = lax.broadcasted_iota(jnp.int32, (ROWS, 128), 1)
    loads[0].wait()
    loads[1].wait()
    e_side, p_side = raw[0, mid, pl.ds(HALF, 128)], raw[1, mid, pl.ds(HALF, 128)]
    side_x[0] = jnp.where(lanes < 8, pltpu.roll(e_side, 8, axis=1), pltpu.roll(p_side, 16, axis=1))
    e_side, p_side = raw[0, mid, pl.ds(128, 128)], raw[1, mid, pl.ds(128, 128)]
    side_x[1] = jnp.where(lanes < 8, e_side, pltpu.roll(p_side, 8, axis=1))
    for d in (0, 1):
        side_send[d, :, pl.ds(0, ROWS)] = jnp.transpose(side_x[d])[:16]

    pl.semaphore_wait(barrier, 10)

    started = []

    def message(src, dst, to):
        at = len(started)
        assert at < COPIES
        copy = pltpu.make_async_remote_copy(
            src, dst, send_sem.at[at], recv_sem.at[at], device_id=to, device_id_type=MESH
        )
        started.append(copy)
        return copy

    def send(src, dst, to):
        copy = message(src, dst, to)
        copy.start()
        return copy

    raw_copies = []
    for d, db in ((0, 1), (1, -1)):
        raw_copies.append(send(side_send.at[d], side_recv.at[d], device(0, db)))
        for dx, src, dst in ((1, pl.ds(56, 8), pl.ds(0, 8)), (-1, pl.ds(0, 8), pl.ds(72, 8))):
            raw_copies.append(send(side_x.at[d, src], side_in.at[d, dst], device(dx, db)))
    for dx, src, dst in ((1, pl.ds(64, 8), pl.ds(0, 8)), (-1, pl.ds(8, 8), pl.ds(72, 8))):
        raw_copies.append(send(raw.at[:, src, inner], raw.at[:, dst, inner], device(dx, 0)))

    bound_early = send(
        vol_hbm.at[edge, pl.ds(0, EARLY)], vol.at[theirs, pl.ds(8, EARLY), tile], partner
    )
    bound_late = message(
        vol_hbm.at[edge, pl.ds(EARLY, ROWS - EARLY)],
        vol.at[theirs, pl.ds(8 + EARLY, ROWS - EARLY), tile],
        partner,
    )
    side_copies = []
    for by, src, dst in (
        (1, pl.ds(WIDE - 128, 128), pl.ds(0, 128)),
        (-1, pl.ds(0, 128), pl.ds(WIDE + 128, 128)),
    ):
        to = device(0, 2 * by)
        side_copies.append(send(vol_hbm.at[:, :, src], vol.at[pl.ds(1, LAYERS), mid, dst], to))
        side_copies.append(send(seabed_hbm.at[:, src], seabed.at[:, dst], to))

    loads[2].wait()
    loads[3].wait()
    for d, row in ((0, 63), (1, 0)):

        @pl.loop(0, LAYERS)
        def _(k):
            for t in range(16):
                rows_out[d, k, pl.ds(t, 1), :] = vol[
                    k + 1, pl.ds(row + 8, 1), pl.ds(128 + 128 * t, 128)
                ]

        for t in range(16):
            bed = seabed[pl.ds(row, 1), pl.ds(128 + 128 * t, 128)]
            rows_out[d, LAYERS, pl.ds(t, 1), :] = bed.astype(jnp.float32) * DEPTH_UNIT
    row_copies = []
    for d, dx in ((0, 1), (1, -1)):
        row_copies.append(send(rows_out.at[d], rows_in.at[d], device(dx, 0)))
        row_copies.append(send(rows_out.at[d, edge], ring_rows.at[d], device(dx, side)))

    for copy in raw_copies:
        copy.wait_recv()
    for d in (0, 1):
        back = jnp.transpose(side_recv[d])
        side_in[d, mid, pl.ds(0, 16)] = back[:ROWS]
        block_in = side_in[d]
        at = pl.ds(0, 128) if d == 0 else pl.ds(HALF + 128, 128)
        raw[0, :, at] = pltpu.roll(block_in, 120, axis=1) if d == 0 else block_in
        raw[1, :, at] = pltpu.roll(block_in, 112 if d == 0 else 120, axis=1)

    def tiles(ref, lead, r):
        def rows(i):
            return ref[lead + (pl.ds(pl.multiple_of(8 * i, 8), 8), slice(None))]

        return rows(jnp.maximum(r - 1, 0)), rows(r), rows(jnp.minimum(r + 1, 9))

    @pl.loop(0, 10)
    def _(r):
        height, poten = tiles(raw, (0,), r), tiles(raw, (1,), r)
        rate_height, rate_poten = section(height, poten)
        at = pl.ds(pl.multiple_of(8 * r, 8), 8)
        one[0, at, :] = height[1] + TIME_STEP * rate_height
        one[1, at, :] = poten[1] + TIME_STEP * rate_poten

    @pl.loop(0, 10)
    def _(r):
        height, poten = tiles(one, (0,), r), tiles(one, (1,), r)
        rates = section(height, poten)
        at = pl.ds(pl.multiple_of(8 * r, 8), 8)
        for f in (0, 1):
            first = (height, poten)[f][1]
            new[0, f, at, :] = 0.5 * (raw[f, at, :] + first + TIME_STEP * rates[f])

    field_copies = [
        message(new.at[0, f, mid, inner], new.at[1, f, mid, inner], partner) for f in (0, 1)
    ]
    field_copies[0].start()

    @pl.when(gz == 0)
    def _():
        field_copies[1].start()

    for f in (0, 1):
        for d, row in ((0, 7), (1, 72)):
            for t in range(8):
                new_rows_out[f, d, pl.ds(t, 1), :] = new[
                    0, f, pl.ds(row, 1), pl.ds(128 + 128 * t, 128)
                ]
    ring_copies = [send(new_rows_out, new_rows_in, partner)]
    new_e_out[...] = new[0, 0, mid, inner]
    new_p_out[...] = new[0, 1, mid, inner]

    for copy in side_copies:
        copy.wait_recv()
    outer = pl.multiple_of((HALF + 128) * gz, 128)
    left = vol[edge + 1, mid, pl.ds(0, 128)]
    right = vol[edge + 1, mid, pl.ds(WIDE + 128, 128)]
    outer_e = new[0, 0, mid, pl.ds(outer, 128)]
    outer_p = new[0, 1, mid, pl.ds(outer, 128)]

    def pick(x, even, odd):
        return jnp.where(
            gz == 0, pltpu.roll(x, even, axis=1), pltpu.roll(x, odd, axis=1)
        )

    packed = jnp.where(
        lanes < 2,
        jnp.where(lanes == 0, pltpu.roll(left, 1, axis=1), pltpu.roll(right, 1, axis=1)),
        jnp.where(lanes == 2, pick(outer_e, 3, 2), pick(outer_p, 4, 3)),
    )
    cols_out[:, pl.ds(0, ROWS)] = jnp.transpose(packed)[:8]
    ring_copies.append(send(cols_out, cols_in, partner))

    @pl.loop(0, 8)
    def _(r):
        at = pl.multiple_of(8 * r, 8)
        depth[pl.ds(at + 8, 8), :] = seabed[pl.ds(at, 8), :].astype(jnp.float32) * DEPTH_UNIT

    for copy in row_copies:
        copy.wait_recv()
    for d, row in ((0, 7), (1, 72)):

        @pl.loop(0, LAYERS)
        def _(k):
            for t in range(16):
                vol[k + 1, pl.ds(row, 1), pl.ds(128 + 128 * t, 128)] = rows_in[d, k, pl.ds(t, 1), :]

        for t in range(16):
            at = pl.ds(128 + 128 * t, 128)
            depth[pl.ds(row, 1), at] = rows_in[d, LAYERS, pl.ds(t, 1), :]
            vol[mine, pl.ds(row, 1), at] = ring_rows[d, pl.ds(t, 1), :]

    def prepare(h):
        base = pl.multiple_of(HALF * (gz if h == 0 else 1 - gz), 128)
        span = pl.ds(base, HALF + 256)

        @pl.loop(0, 10)
        def _(r):
            at = pl.ds(pl.multiple_of(8 * r, 8), 8)
            column[h, at, :] = depth[at, span] + new[h, 0, at, :]

            @pl.when(gz == 0)
            def _():
                vol[0, at, span] = vol[1, at, span]

            @pl.when(gz == 1)
            def _():
                vol[9, at, span] = 2.0 * new[h, 1, at, :] - vol[8, at, span]

    def laplace(h, start, count, first_tile, last_tile):
        base = HALF * (gz if h == 0 else 1 - gz)
        sigma = ((8 * gz + start).astype(jnp.float32) + 0.5) * 0.0625

        @pl.loop(first_tile, last_tile)
        def _(r):
            row = pl.multiple_of(8 * r + 8, 8)

            @pl.loop(0, HALF // STRIP)
            def _(s):
                lane = pl.multiple_of(s * STRIP, 128)
                full = pl.multiple_of(base + lane, 128)

                def around(ref, lead, lane):
                    def rows(at, lanes):
                        return ref[lead + (pl.ds(at, 8), lanes)]

                    wide = rows(row, pl.ds(lane, STRIP + 256))
                    here = wide[:, 128 : 128 + STRIP]
                    centre = pl.ds(pl.multiple_of(lane + 128, 128), STRIP)
                    before, after = rows(row - 8, centre), rows(row + 8, centre)
                    up = row_shift(before, here, after, 1)
                    down = row_shift(before, here, after, -1)
                    right = lane_shift(wide, 1)[:, 128 : 128 + STRIP]
                    left = lane_shift(wide, -1)[:, 128 : 128 + STRIP]
                    return here, up - down, right - left, (up + down) + (right + left)

                here, column_north, column_east, _ = around(column, (h,), lane)
                _, depth_north, depth_east, _ = around(depth, (), full)
                inverse = 1.0 / here
                scale = 4.0 * inverse
                step_north = column_north * scale
                step_east = column_east * scale
                slope_north = depth_north * scale - sigma * step_north
                slope_east = depth_east * scale - sigma * step_east
                step_north = step_north * 0.0625
                step_east = step_east * 0.0625
                bottom = 64.0 * inverse * inverse
                below = around(vol, (start,), full)
                middle = around(vol, (start + 1,), full)
                for k in range(count):
                    above = around(vol, (start + k + 2,), full)
                    weight = slope_north * slope_north + slope_east * slope_east + bottom
                    four = 4.0 * middle[0]
                    vertical = 4.0 * (above[0] + below[0]) - 2.0 * four
                    lap_ref[start + k, pl.ds(row - 8, 8), pl.ds(full, STRIP)] = (
                        (middle[3] - four)
                        + slope_north * (above[1] - below[1])
                        + slope_east * (above[2] - below[2])
                        + weight * vertical
                    )
                    slope_north = slope_north - step_north
                    slope_east = slope_east - step_east
                    below, middle = middle, above

    prepare(0)
    laplace(0, gz, LAYERS - 1, 0, 8)

    @pl.when(gz == 1)
    def _():
        field_copies[0].wait_send()
        bound_late.start()
        field_copies[1].wait_recv()

    field_copies[0].wait_recv()
    for copy in ring_copies:
        copy.wait_recv()
    for f in (0, 1):
        for d, row in ((0, 7), (1, 72)):
            for t in range(8):
                new[1, f, pl.ds(row, 1), pl.ds(128 + 128 * t, 128)] = new_rows_in[
                    f, d, pl.ds(t, 1), :
                ]
    back = jnp.transpose(cols_in[...])[:ROWS]
    seam = jnp.zeros((ROWS, 128 - 8), jnp.float32)
    back = jnp.concatenate([back, seam], axis=1)
    vol[mine, mid, pl.ds(0, 128)] = pltpu.roll(back, 127, axis=1)
    vol[mine, mid, pl.ds(WIDE + 128, 128)] = pltpu.roll(back, 127, axis=1)
    far = pl.multiple_of((HALF + 128) * (1 - gz), 128)
    close = pl.multiple_of((HALF + 128) * gz, 128)
    inside = pl.multiple_of(HALF * (1 - gz) + 128 * gz, 128)
    for f in (0, 1):
        new[1, f, mid, pl.ds(far, 128)] = pick(back, 126 - f, 125 - f)
        new[1, f, mid, pl.ds(close, 128)] = new[0, f, mid, pl.ds(inside, 128)]

    prepare(1)
    laplace(1, gz, LAYERS - 1, 0, 8)

    @pl.when(gz == 0)
    def _():
        field_copies[0].wait_send()
        field_copies[1].wait_send()
        bound_late.start()

    bound_early.wait_recv()
    split = EARLY // 8 - 1
    for h in (0, 1):
        laplace(h, edge, 1, 0, split)
    bound_late.wait_recv()
    for h in (0, 1):
        laplace(h, edge, 1, split, 8)

    for copy in started:
        if all(copy is not other for other in field_copies):
            copy.wait_send()


def write(e_ref, p_ref, lap_ref, e_out, p_out, lap_out, sem):
    copies = [
        pltpu.make_async_copy(src, dst, sem.at[i])
        for i, (src, dst) in enumerate(((lap_ref, lap_out), (e_ref, e_out), (p_ref, p_out)))
    ]
    for copy in copies:
        copy.start()
    for copy in copies:
        copy.wait()


def shards(elevation, surface_potential, seabed, interior_potential):
    hbm = pl.BlockSpec(memory_space=pltpu.HBM)
    vmem = pl.BlockSpec(memory_space=pltpu.VMEM)
    f32 = jnp.float32
    held = (
        pltpu.VMEM((ROWS, HALF), f32),
        pltpu.VMEM((ROWS, HALF), f32),
        pltpu.VMEM((LAYERS, ROWS, WIDE), f32),
    )
    operands = [
        pltpu.with_memory_space_constraint(x, pltpu.HBM)
        for x in (elevation, surface_potential, seabed, interior_potential)
    ]
    results = pl.pallas_call(
        kernel,
        out_shape=held,
        in_specs=[hbm] * 4,
        out_specs=(vmem,) * 3,
        scratch_shapes=[
            pltpu.VMEM((2, ROWS + 16, HALF + 256), f32),
            pltpu.VMEM((2, ROWS + 16, HALF + 256), f32),
            pltpu.VMEM((2, 2, ROWS + 16, HALF + 256), f32),
            pltpu.VMEM((ROWS, WIDE + 256), jnp.int32),
            pltpu.VMEM((LAYERS + 2, ROWS + 16, WIDE + 256), f32),
            pltpu.VMEM((ROWS + 16, WIDE + 256), f32),
            pltpu.VMEM((2, ROWS + 16, HALF + 256), f32),
            pltpu.VMEM((2, ROWS, 128), f32),
            pltpu.VMEM((2, 16, 128), f32),
            pltpu.VMEM((2, 16, 128), f32),
            pltpu.VMEM((2, ROWS + 16, 128), f32),
            pltpu.VMEM((2, LAYERS + 1, 16, 128), f32),
            pltpu.VMEM((2, LAYERS + 1, 16, 128), f32),
            pltpu.VMEM((2, 16, 128), f32),
            pltpu.VMEM((2, 2, 8, 128), f32),
            pltpu.VMEM((2, 2, 8, 128), f32),
            pltpu.VMEM((8, 128), f32),
            pltpu.VMEM((8, 128), f32),
            pltpu.SemaphoreType.DMA((4,)),
            pltpu.SemaphoreType.DMA((COPIES,)),
            pltpu.SemaphoreType.DMA((COPIES,)),
        ],
        compiler_params=pltpu.CompilerParams(
            collective_id=0, has_side_effects=True, vmem_limit_bytes=40 << 20
        ),
        name="wave_step",
    )(*operands)
    return pl.pallas_call(
        write,
        out_shape=tuple(jax.ShapeDtypeStruct(x.shape, f32) for x in results),
        in_specs=[vmem] * 3,
        out_specs=(hbm,) * 3,
        scratch_shapes=[pltpu.SemaphoreType.DMA((3,))],
        compiler_params=pltpu.CompilerParams(vmem_limit_bytes=4 << 20),
        name="write_results",
    )(*(pltpu.with_memory_space_constraint(x, pltpu.VMEM) for x in results))


def solution(mesh):
    return jax.shard_map(
        shards,
        mesh=mesh,
        in_specs=(P("gx", ("gy", "gz")), P("gx", ("gy", "gz")), P("gx", "gy"), P("gz", "gx", "gy")),
        out_specs=(P("gx", ("gy", "gz")), P("gx", ("gy", "gz")), P("gz", "gx", "gy")),
        check_vma=False,
    )
```

```python
import jax
import jax.numpy as jnp
from jax import lax
from jax.experimental import pallas as pl
from jax.experimental.pallas import tpu as pltpu
from jax.sharding import PartitionSpec as P

MESH = pl.DeviceIdType.MESH
TIME_STEP = 0.05
DEPTH_UNIT = 0.015625

ROWS = 64
HALF = 1024
WIDE = 2048
LAYERS = 8
STRIP = 1024
EARLY = 40
COPIES = 32


def lane_shift(x, by):
    return pltpu.roll(x, (-by) % x.shape[-1], axis=len(x.shape) - 1)


def row_shift(before, here, after, by):
    rows = lax.broadcasted_iota(jnp.int32, here.shape, 0)
    moved = pltpu.roll(here, (-by) % 8, axis=0)
    if by > 0:
        return jnp.where(rows >= 8 - by, pltpu.roll(after, 8 - by, axis=0), moved)
    return jnp.where(rows < -by, pltpu.roll(before, -by, axis=0), moved)


def section(height, poten):
    def parts(tiles):
        before, here, after = tiles
        north = [row_shift(before, here, after, by) for by in (-2, -1, 1, 2)]
        east = [lane_shift(here, by) for by in (-2, -1, 1, 2)]
        return north, east

    def first(m2, m1, p1, p2):
        return 8.0 * (p1 - m1) - (p2 - m2)

    height_north, height_east = parts(height)
    poten_north, poten_east = parts(poten)
    e_n, e_e = first(*height_north), first(*height_east)
    p_n, p_e = first(*poten_north), first(*poten_east)
    near = (poten_north[1] + poten_north[2]) + (poten_east[1] + poten_east[2])
    far = (poten_north[0] + poten_north[3]) + (poten_east[0] + poten_east[3])
    curve = 16.0 * near - far - 60.0 * poten[1]
    rate_height = curve * (1.0 / 12.0) - (e_n * p_n + e_e * p_e) * (1.0 / 144.0)
    rate_poten = -height[1] - (p_n * p_n + p_e * p_e) * (0.5 / 144.0)
    return rate_height, rate_poten


def kernel(
    e_hbm, p_hbm, seabed_hbm, vol_hbm,
    new_e_out, new_p_out, lap_ref,
    raw, one, new, seabed, vol, depth, column,
    side_x, side_send, side_recv, side_in, relay, relay_two,
    rows_out, rows_in, ring_rows, new_rows_out, new_rows_in, cols_out, cols_in,
    local_sem, send_sem, recv_sem,
):
    gx, gy, gz = lax.axis_index("gx"), lax.axis_index("gy"), lax.axis_index("gz")
    block = 2 * gy + gz

    def device(dx, db):
        at = lax.rem(block + db + 8, 8)
        return (lax.rem(gx + dx + 32, 32), lax.div(at, 2), lax.rem(at, 2))

    side = 1 - 2 * gz
    partner = (gx, gy, 1 - gz)
    opposite = (lax.rem(gx + 16, 32), gy, 1 - gz)
    theirs = 9 * gz
    mine = 9 - theirs
    edge = 7 * (1 - gz)
    mid = pl.ds(8, ROWS)
    inner = pl.ds(128, HALF)
    tile = pl.ds(128, WIDE)

    loads = [
        pltpu.make_async_copy(e_hbm, raw.at[0, mid, inner], local_sem.at[0]),
        pltpu.make_async_copy(p_hbm, raw.at[1, mid, inner], local_sem.at[1]),
        pltpu.make_async_copy(seabed_hbm, seabed.at[:, tile], local_sem.at[2]),
        pltpu.make_async_copy(vol_hbm, vol.at[pl.ds(1, LAYERS), mid, tile], local_sem.at[3]),
    ]
    for load in loads:
        load.start()

    barrier = pltpu.get_barrier_semaphore()
    corners = [(-1, -1), (-1, 1), (1, -1), (1, 1)]
    for dx, db in corners + [(-1, 0), (1, 0), (0, -1), (0, 1), (0, -2), (0, 2)]:
        pl.semaphore_signal(barrier, inc=1, device_id=device(dx, db), device_id_type=MESH)
    pl.semaphore_signal(barrier, inc=1, device_id=opposite, device_id_type=MESH)

    lanes = lax.broadcasted_iota(jnp.int32, (ROWS, 128), 1)
    loads[0].wait()
    loads[1].wait()
    e_side, p_side = raw[0, mid, pl.ds(HALF, 128)], raw[1, mid, pl.ds(HALF, 128)]
    side_x[0] = jnp.where(lanes < 8, pltpu.roll(e_side, 8, axis=1), pltpu.roll(p_side, 16, axis=1))
    e_side, p_side = raw[0, mid, pl.ds(128, 128)], raw[1, mid, pl.ds(128, 128)]
    side_x[1] = jnp.where(lanes < 8, e_side, pltpu.roll(p_side, 8, axis=1))
    for d in (0, 1):
        side_send[d, :, pl.ds(0, ROWS)] = jnp.transpose(side_x[d])[:16]

    pl.semaphore_wait(barrier, 11)

    started, made = [], []

    def message(src, dst, to):
        at = len(made)
        assert at < COPIES
        copy = pltpu.make_async_remote_copy(
            src, dst, send_sem.at[at], recv_sem.at[at], device_id=to, device_id_type=MESH
        )
        made.append(copy)
        return copy

    def send(src, dst, to):
        copy = message(src, dst, to)
        copy.start()
        started.append(copy)
        return copy


    raw_copies = []
    for d, db in ((0, 1), (1, -1)):
        raw_copies.append(send(side_send.at[d], side_recv.at[d], device(0, db)))
        for dx, src, dst in ((1, pl.ds(56, 8), pl.ds(0, 8)), (-1, pl.ds(0, 8), pl.ds(72, 8))):
            raw_copies.append(send(side_x.at[d, src], side_in.at[d, dst], device(dx, db)))
    for dx, src, dst in ((1, pl.ds(64, 8), pl.ds(0, 8)), (-1, pl.ds(8, 8), pl.ds(72, 8))):
        raw_copies.append(send(raw.at[:, src, inner], raw.at[:, dst, inner], device(dx, 0)))

    rest = pl.ds(EARLY, ROWS - EARLY)
    rest_in = pl.ds(8 + EARLY, ROWS - EARLY)
    bound_early = send(
        vol_hbm.at[edge, pl.ds(0, EARLY)], vol.at[theirs, pl.ds(8, EARLY), tile], partner
    )
    bound_late = message(vol_hbm.at[0, rest], vol.at[9, rest_in, tile], partner)
    hops = [
        message(vol_hbm.at[7, rest], relay, opposite),
        message(relay, relay_two, partner),
        message(relay_two, vol.at[0, rest_in, tile], opposite),
    ]

    @pl.when(gz == 0)
    def _():
        hops[0].start()

    side_copies = []
    for by, src, dst in (
        (1, pl.ds(WIDE - 128, 128), pl.ds(0, 128)),
        (-1, pl.ds(0, 128), pl.ds(WIDE + 128, 128)),
    ):
        to = device(0, 2 * by)
        side_copies.append(send(vol_hbm.at[:, :, src], vol.at[pl.ds(1, LAYERS), mid, dst], to))
        side_copies.append(send(seabed_hbm.at[:, src], seabed.at[:, dst], to))

    loads[2].wait()
    loads[3].wait()
    for d, row in ((0, 63), (1, 0)):

        @pl.loop(0, LAYERS)
        def _(k):
            for t in range(16):
                rows_out[d, k, pl.ds(t, 1), :] = vol[
                    k + 1, pl.ds(row + 8, 1), pl.ds(128 + 128 * t, 128)
                ]

        for t in range(16):
            bed = seabed[pl.ds(row, 1), pl.ds(128 + 128 * t, 128)]
            rows_out[d, LAYERS, pl.ds(t, 1), :] = bed.astype(jnp.float32) * DEPTH_UNIT
    row_copies = []
    for d, dx in ((0, 1), (1, -1)):
        row_copies.append(send(rows_out.at[d], rows_in.at[d], device(dx, 0)))
        row_copies.append(send(rows_out.at[d, edge], ring_rows.at[d], device(dx, side)))

    for copy in raw_copies:
        copy.wait_recv()
    for d in (0, 1):
        back = jnp.transpose(side_recv[d])
        side_in[d, mid, pl.ds(0, 16)] = back[:ROWS]
        block_in = side_in[d]
        at = pl.ds(0, 128) if d == 0 else pl.ds(HALF + 128, 128)
        raw[0, :, at] = pltpu.roll(block_in, 120, axis=1) if d == 0 else block_in
        raw[1, :, at] = pltpu.roll(block_in, 112 if d == 0 else 120, axis=1)

    def tiles(ref, lead, r):
        def rows(i):
            return ref[lead + (pl.ds(pl.multiple_of(8 * i, 8), 8), slice(None))]

        return rows(jnp.maximum(r - 1, 0)), rows(r), rows(jnp.minimum(r + 1, 9))

    @pl.loop(0, 10)
    def _(r):
        height, poten = tiles(raw, (0,), r), tiles(raw, (1,), r)
        rate_height, rate_poten = section(height, poten)
        at = pl.ds(pl.multiple_of(8 * r, 8), 8)
        one[0, at, :] = height[1] + TIME_STEP * rate_height
        one[1, at, :] = poten[1] + TIME_STEP * rate_poten

    @pl.when(gz == 1)
    def _():
        hops[0].wait_recv()
        hops[1].start()

    @pl.loop(0, 10)
    def _(r):
        height, poten = tiles(one, (0,), r), tiles(one, (1,), r)
        rates = section(height, poten)
        at = pl.ds(pl.multiple_of(8 * r, 8), 8)
        for f in (0, 1):
            first = (height, poten)[f][1]
            new[0, f, at, :] = 0.5 * (raw[f, at, :] + first + TIME_STEP * rates[f])

    field_copies = [
        message(new.at[0, f, mid, inner], new.at[1, f, mid, inner], partner) for f in (0, 1)
    ]
    field_copies[0].start()

    for f in (0, 1):
        for d, row in ((0, 7), (1, 72)):
            for t in range(8):
                new_rows_out[f, d, pl.ds(t, 1), :] = new[
                    0, f, pl.ds(row, 1), pl.ds(128 + 128 * t, 128)
                ]
    ring_copies = [send(new_rows_out, new_rows_in, partner)]
    new_e_out[...] = new[0, 0, mid, inner]
    new_p_out[...] = new[0, 1, mid, inner]

    for copy in side_copies:
        copy.wait_recv()
    outer = pl.multiple_of((HALF + 128) * gz, 128)
    left = vol[edge + 1, mid, pl.ds(0, 128)]
    right = vol[edge + 1, mid, pl.ds(WIDE + 128, 128)]
    outer_e = new[0, 0, mid, pl.ds(outer, 128)]
    outer_p = new[0, 1, mid, pl.ds(outer, 128)]

    def pick(x, even, odd):
        return jnp.where(
            gz == 0, pltpu.roll(x, even, axis=1), pltpu.roll(x, odd, axis=1)
        )

    packed = jnp.where(
        lanes < 2,
        jnp.where(lanes == 0, pltpu.roll(left, 1, axis=1), pltpu.roll(right, 1, axis=1)),
        jnp.where(lanes == 2, pick(outer_e, 3, 2), pick(outer_p, 4, 3)),
    )
    cols_out[:, pl.ds(0, ROWS)] = jnp.transpose(packed)[:8]
    ring_copies.append(send(cols_out, cols_in, partner))

    @pl.loop(0, 8)
    def _(r):
        at = pl.multiple_of(8 * r, 8)
        depth[pl.ds(at + 8, 8), :] = seabed[pl.ds(at, 8), :].astype(jnp.float32) * DEPTH_UNIT

    for copy in row_copies:
        copy.wait_recv()
    for d, row in ((0, 7), (1, 72)):

        @pl.loop(0, LAYERS)
        def _(k):
            for t in range(16):
                vol[k + 1, pl.ds(row, 1), pl.ds(128 + 128 * t, 128)] = rows_in[d, k, pl.ds(t, 1), :]

        for t in range(16):
            at = pl.ds(128 + 128 * t, 128)
            depth[pl.ds(row, 1), at] = rows_in[d, LAYERS, pl.ds(t, 1), :]

    def prepare(h, do_column, do_top):
        base = pl.multiple_of(HALF * (gz if h == 0 else 1 - gz), 128)
        span = pl.ds(base, HALF + 256)

        @pl.loop(0, 10)
        def _(r):
            at = pl.ds(pl.multiple_of(8 * r, 8), 8)
            if do_column:
                column[h, at, :] = depth[at, span] + new[h, 0, at, :]

                @pl.when(gz == 0)
                def _():
                    vol[0, at, span] = vol[1, at, span]

            if do_top:

                @pl.when(gz == 1)
                def _():
                    vol[9, at, span] = 2.0 * new[h, 1, at, :] - vol[8, at, span]

    def laplace(h, start, count, first_tile, last_tile):
        base = HALF * (gz if h == 0 else 1 - gz)
        sigma = ((8 * gz + start).astype(jnp.float32) + 0.5) * 0.0625

        @pl.loop(first_tile, last_tile)
        def _(r):
            row = pl.multiple_of(8 * r + 8, 8)

            @pl.loop(0, HALF // STRIP)
            def _(s):
                lane = pl.multiple_of(s * STRIP, 128)
                full = pl.multiple_of(base + lane, 128)

                def around(ref, lead, lane):
                    def rows(at, lanes):
                        return ref[lead + (pl.ds(at, 8), lanes)]

                    wide = rows(row, pl.ds(lane, STRIP + 256))
                    here = wide[:, 128 : 128 + STRIP]
                    centre = pl.ds(pl.multiple_of(lane + 128, 128), STRIP)
                    before, after = rows(row - 8, centre), rows(row + 8, centre)
                    up = row_shift(before, here, after, 1)
                    down = row_shift(before, here, after, -1)
                    right = lane_shift(wide, 1)[:, 128 : 128 + STRIP]
                    left = lane_shift(wide, -1)[:, 128 : 128 + STRIP]
                    return here, up - down, right - left, (up + down) + (right + left)

                here, column_north, column_east, _ = around(column, (h,), lane)
                _, depth_north, depth_east, _ = around(depth, (), full)
                inverse = 1.0 / here
                scale = 4.0 * inverse
                step_north = column_north * scale
                step_east = column_east * scale
                slope_north = depth_north * scale - sigma * step_north
                slope_east = depth_east * scale - sigma * step_east
                step_north = step_north * 0.0625
                step_east = step_east * 0.0625
                bottom = 64.0 * inverse * inverse
                below = around(vol, (start,), full)
                middle = around(vol, (start + 1,), full)
                for k in range(count):
                    above = around(vol, (start + k + 2,), full)
                    weight = slope_north * slope_north + slope_east * slope_east + bottom
                    four = 4.0 * middle[0]
                    vertical = 4.0 * (above[0] + below[0]) - 2.0 * four
                    lap_ref[start + k, pl.ds(row - 8, 8), pl.ds(full, STRIP)] = (
                        (middle[3] - four)
                        + slope_north * (above[1] - below[1])
                        + slope_east * (above[2] - below[2])
                        + weight * vertical
                    )
                    slope_north = slope_north - step_north
                    slope_east = slope_east - step_east
                    below, middle = middle, above

    prepare(0, True, True)
    laplace(0, gz, LAYERS - 1, 0, 8)

    @pl.when(gz == 0)
    def _():
        field_copies[1].start()
        hops[1].wait_recv()
        hops[2].start()

    for copy in ring_copies:
        copy.wait_recv()
    for d, row in ((0, 7), (1, 72)):
        for t in range(16):
            vol[mine, pl.ds(row, 1), pl.ds(128 + 128 * t, 128)] = ring_rows[d, pl.ds(t, 1), :]
        for f in (0, 1):
            for t in range(8):
                new[1, f, pl.ds(row, 1), pl.ds(128 + 128 * t, 128)] = new_rows_in[
                    f, d, pl.ds(t, 1), :
                ]
    back = jnp.transpose(cols_in[...])[:ROWS]
    back = jnp.concatenate([back, jnp.zeros((ROWS, 128 - 8), jnp.float32)], axis=1)
    vol[mine, mid, pl.ds(0, 128)] = pltpu.roll(back, 127, axis=1)
    vol[mine, mid, pl.ds(WIDE + 128, 128)] = pltpu.roll(back, 127, axis=1)
    far = pl.multiple_of((HALF + 128) * (1 - gz), 128)
    close = pl.multiple_of((HALF + 128) * gz, 128)
    inside = pl.multiple_of(HALF * (1 - gz) + 128 * gz, 128)
    for f in (0, 1):
        new[1, f, mid, pl.ds(far, 128)] = pick(back, 126 - f, 125 - f)
        new[1, f, mid, pl.ds(close, 128)] = new[0, f, mid, pl.ds(inside, 128)]

    bound_early.wait_recv()
    split = EARLY // 8 - 1
    laplace(0, edge, 1, 0, split)

    @pl.when(gz == 1)
    def _():
        field_copies[0].wait_send()
        bound_late.start()

    field_copies[0].wait_recv()
    prepare(1, True, False)

    @pl.when(gz == 0)
    def _():
        laplace(1, 0, LAYERS - 1, 0, 8)
        laplace(1, LAYERS - 1, 1, 0, split)
        bound_late.wait_recv()
        for h in (0, 1):
            laplace(h, LAYERS - 1, 1, split, 8)

    @pl.when(gz == 1)
    def _():
        laplace(1, 1, LAYERS - 2, 0, 8)
        laplace(1, 0, 1, 0, split)
        hops[2].wait_recv()
        for h in (0, 1):
            laplace(h, 0, 1, split, 8)
        field_copies[1].wait_recv()
        prepare(1, False, True)
        laplace(1, LAYERS - 1, 1, 0, 8)

    @pl.when(gz == 0)
    def _():
        for copy in (*field_copies, hops[0], hops[2]):
            copy.wait_send()

    @pl.when(gz == 1)
    def _():
        for copy in (hops[1], bound_late):
            copy.wait_send()

    for copy in started:
        copy.wait_send()


def write(e_ref, p_ref, lap_ref, e_out, p_out, lap_out, sem):
    copies = [
        pltpu.make_async_copy(src, dst, sem.at[i])
        for i, (src, dst) in enumerate(((lap_ref, lap_out), (e_ref, e_out), (p_ref, p_out)))
    ]
    for copy in copies:
        copy.start()
    for copy in copies:
        copy.wait()


def shards(elevation, surface_potential, seabed, interior_potential):
    hbm = pl.BlockSpec(memory_space=pltpu.HBM)
    vmem = pl.BlockSpec(memory_space=pltpu.VMEM)
    f32 = jnp.float32
    held = (
        pltpu.VMEM((ROWS, HALF), f32),
        pltpu.VMEM((ROWS, HALF), f32),
        pltpu.VMEM((LAYERS, ROWS, WIDE), f32),
    )
    operands = [
        pltpu.with_memory_space_constraint(x, pltpu.HBM)
        for x in (elevation, surface_potential, seabed, interior_potential)
    ]
    results = pl.pallas_call(
        kernel,
        out_shape=held,
        in_specs=[hbm] * 4,
        out_specs=(vmem,) * 3,
        scratch_shapes=[
            pltpu.VMEM((2, ROWS + 16, HALF + 256), f32),
            pltpu.VMEM((2, ROWS + 16, HALF + 256), f32),
            pltpu.VMEM((2, 2, ROWS + 16, HALF + 256), f32),
            pltpu.VMEM((ROWS, WIDE + 256), jnp.int32),
            pltpu.VMEM((LAYERS + 2, ROWS + 16, WIDE + 256), f32),
            pltpu.VMEM((ROWS + 16, WIDE + 256), f32),
            pltpu.VMEM((2, ROWS + 16, HALF + 256), f32),
            pltpu.VMEM((2, ROWS, 128), f32),
            pltpu.VMEM((2, 16, 128), f32),
            pltpu.VMEM((2, 16, 128), f32),
            pltpu.VMEM((2, ROWS + 16, 128), f32),
            pltpu.VMEM((ROWS - EARLY, WIDE), f32),
            pltpu.VMEM((ROWS - EARLY, WIDE), f32),
            pltpu.VMEM((2, LAYERS + 1, 16, 128), f32),
            pltpu.VMEM((2, LAYERS + 1, 16, 128), f32),
            pltpu.VMEM((2, 16, 128), f32),
            pltpu.VMEM((2, 2, 8, 128), f32),
            pltpu.VMEM((2, 2, 8, 128), f32),
            pltpu.VMEM((8, 128), f32),
            pltpu.VMEM((8, 128), f32),
            pltpu.SemaphoreType.DMA((4,)),
            pltpu.SemaphoreType.DMA((COPIES,)),
            pltpu.SemaphoreType.DMA((COPIES,)),
        ],
        compiler_params=pltpu.CompilerParams(
            collective_id=0, has_side_effects=True, vmem_limit_bytes=40 << 20
        ),
        name="wave_step",
    )(*operands)
    return pl.pallas_call(
        write,
        out_shape=tuple(jax.ShapeDtypeStruct(x.shape, f32) for x in results),
        in_specs=[vmem] * 3,
        out_specs=(hbm,) * 3,
        scratch_shapes=[pltpu.SemaphoreType.DMA((3,))],
        compiler_params=pltpu.CompilerParams(vmem_limit_bytes=4 << 20),
        name="write_results",
    )(*(pltpu.with_memory_space_constraint(x, pltpu.VMEM) for x in results))


def solution(mesh):
    return jax.shard_map(
        shards,
        mesh=mesh,
        in_specs=(P("gx", ("gy", "gz")), P("gx", ("gy", "gz")), P("gx", "gy"), P("gz", "gx", "gy")),
        out_specs=(P("gx", ("gy", "gz")), P("gx", ("gy", "gz")), P("gz", "gx", "gy")),
        check_vma=False,
    )
```

```python
import jax
import jax.numpy as jnp
from jax import lax
from jax.experimental import pallas as pl
from jax.experimental.pallas import tpu as pltpu
from jax.sharding import PartitionSpec as P

MESH = pl.DeviceIdType.MESH
TIME_STEP = 0.05
DEPTH_UNIT = 0.015625

ROWS = 64
HALF = 1024
WIDE = 2048
LAYERS = 8
STRIP = 512
FIRST = 24
DIRECT = 48
COPIES = 32


def lane_shift(x, by):
    return pltpu.roll(x, (-by) % x.shape[-1], axis=len(x.shape) - 1)


def row_shift(before, here, after, by):
    rows = lax.broadcasted_iota(jnp.int32, here.shape, 0)
    moved = pltpu.roll(here, (-by) % 8, axis=0)
    if by > 0:
        return jnp.where(rows >= 8 - by, pltpu.roll(after, 8 - by, axis=0), moved)
    return jnp.where(rows < -by, pltpu.roll(before, -by, axis=0), moved)


def section(height, poten):
    def parts(tiles):
        before, here, after = tiles
        north = [row_shift(before, here, after, by) for by in (-2, -1, 1, 2)]
        east = [lane_shift(here, by) for by in (-2, -1, 1, 2)]
        return north, east

    def first(m2, m1, p1, p2):
        return 8.0 * (p1 - m1) - (p2 - m2)

    height_north, height_east = parts(height)
    poten_north, poten_east = parts(poten)
    e_n, e_e = first(*height_north), first(*height_east)
    p_n, p_e = first(*poten_north), first(*poten_east)
    near = (poten_north[1] + poten_north[2]) + (poten_east[1] + poten_east[2])
    far = (poten_north[0] + poten_north[3]) + (poten_east[0] + poten_east[3])
    curve = 16.0 * near - far - 60.0 * poten[1]
    rate_height = curve * (1.0 / 12.0) - (e_n * p_n + e_e * p_e) * (1.0 / 144.0)
    rate_poten = -height[1] - (p_n * p_n + p_e * p_e) * (0.5 / 144.0)
    return rate_height, rate_poten


def kernel(
    e_hbm, p_hbm, seabed_hbm, vol_hbm,
    new_e_out, new_p_out, lap_ref,
    raw, one, new, seabed, vol, depth, column, north, east, coef,
    side_x, side_send, side_recv, side_in, relay, relay_two,
    rows_out, rows_in, ring_rows, new_rows_out, new_rows_in, cols_out, cols_in,
    local_sem, send_sem, recv_sem,
):
    gx, gy, gz = lax.axis_index("gx"), lax.axis_index("gy"), lax.axis_index("gz")
    block = 2 * gy + gz

    def device(dx, db):
        at = lax.rem(block + db + 8, 8)
        return (lax.rem(gx + dx + 32, 32), lax.div(at, 2), lax.rem(at, 2))

    side = 1 - 2 * gz
    partner = (gx, gy, 1 - gz)
    opposite = (lax.rem(gx + 16, 32), gy, 1 - gz)
    theirs = 9 * gz
    mine = 9 - theirs
    edge = 7 * (1 - gz)
    mid = pl.ds(8, ROWS)
    inner = pl.ds(128, HALF)
    tile = pl.ds(128, WIDE)

    loads = [
        pltpu.make_async_copy(e_hbm, raw.at[0, mid, inner], local_sem.at[0]),
        pltpu.make_async_copy(p_hbm, raw.at[1, mid, inner], local_sem.at[1]),
        pltpu.make_async_copy(seabed_hbm, seabed.at[:, tile], local_sem.at[2]),
        pltpu.make_async_copy(vol_hbm, vol.at[pl.ds(1, LAYERS), mid, tile], local_sem.at[3]),
    ]
    for load in loads:
        load.start()

    barrier = pltpu.get_barrier_semaphore()
    corners = [(-1, -1), (-1, 1), (1, -1), (1, 1)]
    for dx, db in corners + [(-1, 0), (1, 0), (0, -1), (0, 1), (0, -2), (0, 2)]:
        pl.semaphore_signal(barrier, inc=1, device_id=device(dx, db), device_id_type=MESH)
    pl.semaphore_signal(barrier, inc=1, device_id=opposite, device_id_type=MESH)

    lanes = lax.broadcasted_iota(jnp.int32, (ROWS, 128), 1)
    loads[0].wait()
    loads[1].wait()
    e_side, p_side = raw[0, mid, pl.ds(HALF, 128)], raw[1, mid, pl.ds(HALF, 128)]
    side_x[0] = jnp.where(lanes < 8, pltpu.roll(e_side, 8, axis=1), pltpu.roll(p_side, 16, axis=1))
    e_side, p_side = raw[0, mid, pl.ds(128, 128)], raw[1, mid, pl.ds(128, 128)]
    side_x[1] = jnp.where(lanes < 8, e_side, pltpu.roll(p_side, 8, axis=1))
    for d in (0, 1):
        side_send[d, :, pl.ds(0, ROWS)] = jnp.transpose(side_x[d])[:16]

    pl.semaphore_wait(barrier, 11)

    started, made = [], []

    def message(src, dst, to):
        at = len(made)
        assert at < COPIES
        copy = pltpu.make_async_remote_copy(
            src, dst, send_sem.at[at], recv_sem.at[at], device_id=to, device_id_type=MESH
        )
        made.append(copy)
        return copy

    def send(src, dst, to):
        copy = message(src, dst, to)
        copy.start()
        started.append(copy)
        return copy


    row_halos, side_halos = [], []
    for dx, src, dst in ((1, pl.ds(64, 8), pl.ds(0, 8)), (-1, pl.ds(8, 8), pl.ds(72, 8))):
        row_halos.append(send(raw.at[:, src, inner], raw.at[:, dst, inner], device(dx, 0)))
    for d, db in ((0, 1), (1, -1)):
        side_halos.append(send(side_send.at[d], side_recv.at[d], device(0, db)))
        for dx, src, dst in ((1, pl.ds(56, 8), pl.ds(0, 8)), (-1, pl.ds(0, 8), pl.ds(72, 8))):
            row_halos.append(send(side_x.at[d, src], side_in.at[d, dst], device(dx, db)))

    last = pl.ds(DIRECT, ROWS - DIRECT)
    last_in = pl.ds(8 + DIRECT, ROWS - DIRECT)
    hops = [
        message(vol_hbm.at[7, last], relay, opposite),
        message(relay, relay_two, partner),
        message(relay_two, vol.at[0, last_in, tile], opposite),
    ]

    @pl.when(gz == 0)
    def _():
        hops[0].start()

    loads[2].wait()
    loads[3].wait()
    for d, row in ((0, 63), (1, 0)):

        @pl.loop(0, LAYERS)
        def _(k):
            for t in range(16):
                rows_out[d, k, pl.ds(t, 1), :] = vol[
                    k + 1, pl.ds(row + 8, 1), pl.ds(128 + 128 * t, 128)
                ]

        for t in range(16):
            bed = seabed[pl.ds(row, 1), pl.ds(128 + 128 * t, 128)]
            rows_out[d, LAYERS, pl.ds(t, 1), :] = bed.astype(jnp.float32) * DEPTH_UNIT
    row_copies = []
    for d, dx in ((0, 1), (1, -1)):
        row_copies.append(send(rows_out.at[d], rows_in.at[d], device(dx, 0)))
        row_copies.append(send(rows_out.at[d, edge], ring_rows.at[d], device(dx, side)))

    bound_first = send(
        vol_hbm.at[edge, pl.ds(0, FIRST)], vol.at[theirs, pl.ds(8, FIRST), tile], partner
    )
    bound_next = message(
        vol_hbm.at[7, pl.ds(FIRST, DIRECT - FIRST)],
        vol.at[0, pl.ds(8 + FIRST, DIRECT - FIRST), tile],
        partner,
    )
    bound_late = message(
        vol_hbm.at[0, pl.ds(FIRST, ROWS - FIRST)],
        vol.at[9, pl.ds(8 + FIRST, ROWS - FIRST), tile],
        partner,
    )

    @pl.when(gz == 0)
    def _():
        bound_next.start()

    side_copies = []
    for by, src, dst in (
        (1, pl.ds(WIDE - 128, 128), pl.ds(0, 128)),
        (-1, pl.ds(0, 128), pl.ds(WIDE + 128, 128)),
    ):
        to = device(0, 2 * by)
        side_copies.append(send(vol_hbm.at[:, :, src], vol.at[pl.ds(1, LAYERS), mid, dst], to))
        side_copies.append(send(seabed_hbm.at[:, src], seabed.at[:, dst], to))

    def place_sides(rows):
        for d in (0, 1):
            block_in = side_in[d, rows, :]
            at = pl.ds(0, 128) if d == 0 else pl.ds(HALF + 128, 128)
            raw[0, rows, at] = pltpu.roll(block_in, 120, axis=1) if d == 0 else block_in
            raw[1, rows, at] = pltpu.roll(block_in, 112 if d == 0 else 120, axis=1)

    def tiles(ref, lead, r):
        def rows(i):
            return ref[lead + (pl.ds(pl.multiple_of(8 * i, 8), 8), slice(None))]

        return rows(jnp.maximum(r - 1, 0)), rows(r), rows(jnp.minimum(r + 1, 9))

    def first_section(begin, end):
        @pl.loop(begin, end, unroll=True)
        def _(r):
            height, poten = tiles(raw, (0,), r), tiles(raw, (1,), r)
            rate_height, rate_poten = section(height, poten)
            at = pl.ds(pl.multiple_of(8 * r, 8), 8)
            one[0, at, :] = height[1] + TIME_STEP * rate_height
            one[1, at, :] = poten[1] + TIME_STEP * rate_poten

    def second_section(begin, end):
        @pl.loop(begin, end, unroll=True)
        def _(r):
            height, poten = tiles(one, (0,), r), tiles(one, (1,), r)
            rates = section(height, poten)
            at = pl.ds(pl.multiple_of(8 * r, 8), 8)
            for f in (0, 1):
                first = (height, poten)[f][1]
                new[0, f, at, :] = 0.5 * (raw[f, at, :] + first + TIME_STEP * rates[f])

    def field(f, begin, count):
        rows = pl.ds(begin, count)
        return message(new.at[0, f, rows, inner], new.at[1, f, rows, inner], partner)

    height_copies = [field(0, 24, 32), field(0, 8, 16), field(0, 56, 16)]
    poten_copies = [field(1, 8, 32), field(1, 40, 32)]

    for copy in side_halos:
        copy.wait_recv()
    for d in (0, 1):
        side_in[d, mid, pl.ds(0, 16)] = jnp.transpose(side_recv[d])[:ROWS]
    place_sides(mid)
    first_section(2, 8)

    @pl.when(gz == 1)
    def _():
        hops[0].wait_recv()
        hops[1].start()

    second_section(3, 7)
    height_copies[0].start()
    for copy in row_halos:
        copy.wait_recv()
    place_sides(pl.ds(0, 8))
    place_sides(pl.ds(72, 8))
    first_section(0, 2)
    first_section(8, 10)
    second_section(0, 3)
    height_copies[1].start()
    second_section(7, 10)
    height_copies[2].start()

    for f in (0, 1):
        for d, row in ((0, 7), (1, 72)):
            for t in range(8):
                new_rows_out[f, d, pl.ds(t, 1), :] = new[
                    0, f, pl.ds(row, 1), pl.ds(128 + 128 * t, 128)
                ]
    ring_copies = [send(new_rows_out, new_rows_in, partner)]
    new_e_out[...] = new[0, 0, mid, inner]
    new_p_out[...] = new[0, 1, mid, inner]

    for copy in side_copies:
        copy.wait_recv()
    outer = pl.multiple_of((HALF + 128) * gz, 128)
    left = vol[edge + 1, mid, pl.ds(0, 128)]
    right = vol[edge + 1, mid, pl.ds(WIDE + 128, 128)]
    outer_e = new[0, 0, mid, pl.ds(outer, 128)]
    outer_p = new[0, 1, mid, pl.ds(outer, 128)]

    def pick(x, even, odd):
        return jnp.where(
            gz == 0, pltpu.roll(x, even, axis=1), pltpu.roll(x, odd, axis=1)
        )

    packed = jnp.where(
        lanes < 2,
        jnp.where(lanes == 0, pltpu.roll(left, 1, axis=1), pltpu.roll(right, 1, axis=1)),
        jnp.where(lanes == 2, pick(outer_e, 3, 2), pick(outer_p, 4, 3)),
    )
    cols_out[:, pl.ds(0, ROWS)] = jnp.transpose(packed)[:8]
    ring_copies.append(send(cols_out, cols_in, partner))

    @pl.loop(0, 8)
    def _(r):
        at = pl.multiple_of(8 * r, 8)
        depth[pl.ds(at + 8, 8), :] = seabed[pl.ds(at, 8), :].astype(jnp.float32) * DEPTH_UNIT

    for copy in row_copies:
        copy.wait_recv()
    for d, row in ((0, 7), (1, 72)):

        @pl.loop(0, LAYERS)
        def _(k):
            for t in range(16):
                vol[k + 1, pl.ds(row, 1), pl.ds(128 + 128 * t, 128)] = rows_in[d, k, pl.ds(t, 1), :]

        for t in range(16):
            at = pl.ds(128 + 128 * t, 128)
            depth[pl.ds(row, 1), at] = rows_in[d, LAYERS, pl.ds(t, 1), :]

    def start_of(h):
        return HALF * (gz if h == 0 else 1 - gz)

    def around(ref, lead, row, lane):
        def rows(at, lanes):
            return ref[lead + (pl.ds(at, 8), lanes)]

        wide = rows(row, pl.ds(lane, HALF + 256))
        here = wide[:, 128 : 128 + HALF]
        centre = pl.ds(pl.multiple_of(lane + 128, 128), HALF)
        before, after = rows(row - 8, centre), rows(row + 8, centre)
        up, down = row_shift(before, here, after, 1), row_shift(before, here, after, -1)
        right = lane_shift(wide, 1)[:, 128 : 128 + HALF]
        left = lane_shift(wide, -1)[:, 128 : 128 + HALF]
        return here, up - down, right - left, (up + down) + (right + left)

    def difference(layer, r, lane, flat):
        row = pl.multiple_of(8 * r, 8)
        here, by_row, by_lane, total = around(vol, (layer,), pl.multiple_of(row + 8, 8), lane)
        at = (pl.ds(row, 8), pl.ds(lane, HALF))
        north[(layer,) + at] = by_row
        east[(layer,) + at] = by_lane
        if flat:
            lap_ref[(layer - 1,) + at] = total - 4.0 * here

    def differences(layer, h, first_tile, last_tile, flat):
        lane = pl.multiple_of(start_of(h), 128)

        @pl.loop(first_tile, last_tile, unroll=True)
        def _(r):
            difference(layer, r, lane, flat)

    def coefficients(h):
        lane = pl.multiple_of(start_of(h), 128)
        span = pl.ds(lane, HALF + 256)

        @pl.loop(0, 10, unroll=2)
        def _(r):
            at = pl.ds(pl.multiple_of(8 * r, 8), 8)
            column[h, at, :] = depth[at, span] + new[h, 0, at, :]

        @pl.loop(0, 8, unroll=4)
        def _(r):
            row = pl.multiple_of(8 * r, 8)
            inside = pl.multiple_of(row + 8, 8)
            here, column_north, column_east, _ = around(column, (h,), inside, 0)
            _, depth_north, depth_east, _ = around(depth, (), inside, lane)
            inverse = 1.0 / here
            scale = 4.0 * inverse
            at = (pl.ds(row, 8), pl.ds(lane, HALF))
            coef[(0,) + at] = depth_north * scale
            coef[(1,) + at] = column_north * scale
            coef[(2,) + at] = depth_east * scale
            coef[(3,) + at] = column_east * scale
            coef[(4,) + at] = 64.0 * inverse * inverse

    def top(h, begin, end):
        span = pl.ds(pl.multiple_of(start_of(h), 128), HALF + 256)

        @pl.loop(begin, end)
        def _(r):
            at = pl.ds(pl.multiple_of(8 * r, 8), 8)
            vol[9, at, span] = 2.0 * new[h, 1, at, :] - vol[8, at, span]

    def combine(h, start, count, first_tile, last_tile):
        base = start_of(h)
        sigma = (jnp.asarray(8 * gz + start, jnp.int32).astype(jnp.float32) + 0.5) * 0.0625
        lowest = jnp.where(start + gz == 0, 1, start)

        strip = HALF if count == 1 else STRIP

        @pl.loop(first_tile, last_tile, unroll=count == 1)
        def _(r):
            rows = pl.ds(pl.multiple_of(8 * r, 8), 8)
            inside = pl.ds(pl.multiple_of(8 * r + 8, 8), 8)

            @pl.loop(0, HALF // strip)
            def _(s):
                lane = base + s * strip
                at = (rows, pl.ds(pl.multiple_of(lane, 128), strip))
                centre = (inside, pl.ds(pl.multiple_of(lane + 128, 128), strip))

                def load(layer):
                    return (
                        vol[(layer,) + centre], north[(layer,) + at], east[(layer,) + at]
                    )

                step_north, step_east = coef[(1,) + at], coef[(3,) + at]
                slope_north = coef[(0,) + at] - sigma * step_north
                slope_east = coef[(2,) + at] - sigma * step_east
                step_north = step_north * 0.0625
                step_east = step_east * 0.0625
                bottom = coef[(4,) + at]
                below, middle = load(lowest), load(start + 1)
                for k in range(count):
                    above = load(start + k + 2)
                    weight = slope_north * slope_north + slope_east * slope_east + bottom
                    vertical = 4.0 * (above[0] + below[0]) - 8.0 * middle[0]
                    lap_ref[(start + k,) + at] = (
                        lap_ref[(start + k,) + at]
                        + slope_north * (above[1] - below[1])
                        + slope_east * (above[2] - below[2])
                        + weight * vertical
                    )
                    if k < count - 1:
                        slope_north = slope_north - step_north
                        slope_east = slope_east - step_east
                    below, middle = middle, above

    @pl.loop(0, 8)
    def _(r):
        @pl.loop(0, 2)
        def _(s):
            for layer in range(1, LAYERS + 1):
                difference(layer, r, pl.multiple_of(HALF * s, 128), True)

    @pl.when(gz == 0)
    def _():
        for copy in poten_copies:
            copy.start()
        hops[1].wait_recv()
        hops[2].start()

    @pl.when(gz == 1)
    def _():
        bound_late.start()
        top(0, 0, 10)
        differences(9, 0, 0, 8, False)

    coefficients(0)
    combine(0, gz, LAYERS - 1, 0, 8)

    for copy in ring_copies:
        copy.wait_recv()
    for d, row in ((0, 7), (1, 72)):
        for t in range(16):
            vol[mine, pl.ds(row, 1), pl.ds(128 + 128 * t, 128)] = ring_rows[d, pl.ds(t, 1), :]
        for f in (0, 1):
            for t in range(8):
                new[1, f, pl.ds(row, 1), pl.ds(128 + 128 * t, 128)] = new_rows_in[
                    f, d, pl.ds(t, 1), :
                ]
    back = jnp.transpose(cols_in[...])[:ROWS]
    back = jnp.concatenate([back, jnp.zeros((ROWS, 128 - 8), jnp.float32)], axis=1)
    vol[mine, mid, pl.ds(0, 128)] = pltpu.roll(back, 127, axis=1)
    vol[mine, mid, pl.ds(WIDE + 128, 128)] = pltpu.roll(back, 127, axis=1)
    far = pl.multiple_of((HALF + 128) * (1 - gz), 128)
    close = pl.multiple_of((HALF + 128) * gz, 128)
    inside = pl.multiple_of(HALF * (1 - gz) + 128 * gz, 128)
    for f in (0, 1):
        new[1, f, mid, pl.ds(far, 128)] = pick(back, 126 - f, 125 - f)
        new[1, f, mid, pl.ds(close, 128)] = new[0, f, mid, pl.ds(inside, 128)]

    bound_first.wait_recv()

    @pl.when(gz == 1)
    def _():
        bound_next.wait_recv()

    def other_half():
        for copy in height_copies:
            copy.wait_recv()
        coefficients(1)

    @pl.when(gz == 0)
    def _():
        split = FIRST // 8 - 1
        for h in (0, 1):
            differences(9, h, 0, split, False)
        combine(0, LAYERS - 1, 1, 0, split)
        other_half()
        combine(1, 0, LAYERS - 1, 0, 8)
        combine(1, LAYERS - 1, 1, 0, split)
        bound_late.wait_recv()
        for h in (0, 1):
            differences(9, h, split, 8, False)
            combine(h, LAYERS - 1, 1, split, 8)

    @pl.when(gz == 1)
    def _():
        split = DIRECT // 8 - 1
        for h in (0, 1):
            differences(0, h, 0, split, False)
        combine(0, 0, 1, 0, split)
        other_half()
        combine(1, 1, LAYERS - 2, 0, 8)
        combine(1, 0, 1, 0, split)
        hops[2].wait_recv()
        for h in (0, 1):
            differences(0, h, split, 8, False)
            combine(h, 0, 1, split, 8)
        for copy, (begin, end), (first, last) in zip(
            poten_copies, ((0, 5), (5, 10)), ((0, 3), (3, 8))
        ):
            copy.wait_recv()
            top(1, begin, end)
            differences(9, 1, first, last, False)
            combine(1, LAYERS - 1, 1, first, last)

    for copy in height_copies:
        copy.wait_send()

    @pl.when(gz == 0)
    def _():
        for copy in (*poten_copies, bound_next, hops[0], hops[2]):
            copy.wait_send()

    @pl.when(gz == 1)
    def _():
        for copy in (hops[1], bound_late):
            copy.wait_send()

    for copy in started:
        copy.wait_send()


def write(e_ref, p_ref, lap_ref, e_out, p_out, lap_out, sem):
    pairs = [(lap_ref.at[k], lap_out.at[k]) for k in range(LAYERS)]
    pairs += [(e_ref, e_out), (p_ref, p_out)]
    copies = [pltpu.make_async_copy(*pair, sem.at[i]) for i, pair in enumerate(pairs)]
    for copy in copies:
        copy.start()
    for copy in copies:
        copy.wait()


def shards(elevation, surface_potential, seabed, interior_potential):
    hbm = pl.BlockSpec(memory_space=pltpu.HBM)
    vmem = pl.BlockSpec(memory_space=pltpu.VMEM)
    f32 = jnp.float32
    held = (
        pltpu.VMEM((ROWS, HALF), f32),
        pltpu.VMEM((ROWS, HALF), f32),
        pltpu.VMEM((LAYERS, ROWS, WIDE), f32),
    )
    operands = [
        pltpu.with_memory_space_constraint(x, pltpu.HBM)
        for x in (elevation, surface_potential, seabed, interior_potential)
    ]
    results = pl.pallas_call(
        kernel,
        out_shape=held,
        in_specs=[hbm] * 4,
        out_specs=(vmem,) * 3,
        scratch_shapes=[
            pltpu.VMEM((2, ROWS + 16, HALF + 256), f32),
            pltpu.VMEM((2, ROWS + 16, HALF + 256), f32),
            pltpu.VMEM((2, 2, ROWS + 16, HALF + 256), f32),
            pltpu.VMEM((ROWS, WIDE + 256), jnp.int32),
            pltpu.VMEM((LAYERS + 2, ROWS + 16, WIDE + 256), f32),
            pltpu.VMEM((ROWS + 16, WIDE + 256), f32),
            pltpu.VMEM((2, ROWS + 16, HALF + 256), f32),
            pltpu.VMEM((LAYERS + 2, ROWS, WIDE), f32),
            pltpu.VMEM((LAYERS + 2, ROWS, WIDE), f32),
            pltpu.VMEM((5, ROWS, WIDE), f32),
            pltpu.VMEM((2, ROWS, 128), f32),
            pltpu.VMEM((2, 16, 128), f32),
            pltpu.VMEM((2, 16, 128), f32),
            pltpu.VMEM((2, ROWS + 16, 128), f32),
            pltpu.VMEM((ROWS - DIRECT, WIDE), f32),
            pltpu.VMEM((ROWS - DIRECT, WIDE), f32),
            pltpu.VMEM((2, LAYERS + 1, 16, 128), f32),
            pltpu.VMEM((2, LAYERS + 1, 16, 128), f32),
            pltpu.VMEM((2, 16, 128), f32),
            pltpu.VMEM((2, 2, 8, 128), f32),
            pltpu.VMEM((2, 2, 8, 128), f32),
            pltpu.VMEM((8, 128), f32),
            pltpu.VMEM((8, 128), f32),
            pltpu.SemaphoreType.DMA((4,)),
            pltpu.SemaphoreType.DMA((COPIES,)),
            pltpu.SemaphoreType.DMA((COPIES,)),
        ],
        compiler_params=pltpu.CompilerParams(
            collective_id=0, has_side_effects=True, vmem_limit_bytes=48 << 20
        ),
        name="wave_step",
    )(*operands)
    return pl.pallas_call(
        write,
        out_shape=tuple(jax.ShapeDtypeStruct(x.shape, f32) for x in results),
        in_specs=[vmem] * 3,
        out_specs=(hbm,) * 3,
        scratch_shapes=[pltpu.SemaphoreType.DMA((LAYERS + 2,))],
        compiler_params=pltpu.CompilerParams(vmem_limit_bytes=4 << 20),
        name="write_results",
    )(*(pltpu.with_memory_space_constraint(x, pltpu.VMEM) for x in results))


def solution(mesh):
    return jax.shard_map(
        shards,
        mesh=mesh,
        in_specs=(P("gx", ("gy", "gz")), P("gx", ("gy", "gz")), P("gx", "gy"), P("gz", "gx", "gy")),
        out_specs=(P("gx", ("gy", "gz")), P("gx", ("gy", "gz")), P("gz", "gx", "gy")),
        check_vma=False,
    )
```

```python
import jax
import jax.numpy as jnp
from jax import lax
from jax.experimental import pallas as pl
from jax.experimental.pallas import tpu as pltpu
from jax.sharding import PartitionSpec as P

MESH = pl.DeviceIdType.MESH
TIME_STEP = 0.05
DEPTH_UNIT = 0.015625

ROWS = 64
HALF = 1024
WIDE = 2048
LAYERS = 8
STRIP = 512
LATE = 48
FIRST = 32
DIRECT = 48
COPIES = 32


def lane_shift(x, by):
    return pltpu.roll(x, (-by) % x.shape[-1], axis=len(x.shape) - 1)


def row_shift(before, here, after, by):
    rows = lax.broadcasted_iota(jnp.int32, here.shape, 0)
    moved = pltpu.roll(here, (-by) % 8, axis=0)
    if by > 0:
        return jnp.where(rows >= 8 - by, pltpu.roll(after, 8 - by, axis=0), moved)
    return jnp.where(rows < -by, pltpu.roll(before, -by, axis=0), moved)


def section(height, poten):
    def parts(tiles):
        before, here, after = tiles
        north = [row_shift(before, here, after, by) for by in (-2, -1, 1, 2)]
        east = [lane_shift(here, by) for by in (-2, -1, 1, 2)]
        return north, east

    def first(m2, m1, p1, p2):
        return 8.0 * (p1 - m1) - (p2 - m2)

    height_north, height_east = parts(height)
    poten_north, poten_east = parts(poten)
    e_n, e_e = first(*height_north), first(*height_east)
    p_n, p_e = first(*poten_north), first(*poten_east)
    near = (poten_north[1] + poten_north[2]) + (poten_east[1] + poten_east[2])
    far = (poten_north[0] + poten_north[3]) + (poten_east[0] + poten_east[3])
    curve = 16.0 * near - far - 60.0 * poten[1]
    rate_height = curve * (1.0 / 12.0) - (e_n * p_n + e_e * p_e) * (1.0 / 144.0)
    rate_poten = -height[1] - (p_n * p_n + p_e * p_e) * (0.5 / 144.0)
    return rate_height, rate_poten


def kernel(
    e_hbm, p_hbm, seabed_hbm, vol_hbm,
    new_e_out, new_p_out, lap_ref,
    raw, one, new, seabed, vol, depth, column, north, east, coef,
    side_x, side_send, side_recv, side_in, relay, relay_two,
    rows_out, rows_in, ring_rows, new_rows_out, new_rows_in, cols_out, cols_in,
    local_sem, send_sem, recv_sem,
):
    gx, gy, gz = lax.axis_index("gx"), lax.axis_index("gy"), lax.axis_index("gz")
    block = 2 * gy + gz

    def device(dx, db):
        at = lax.rem(block + db + 8, 8)
        return (lax.rem(gx + dx + 32, 32), lax.div(at, 2), lax.rem(at, 2))

    side = 1 - 2 * gz
    partner = (gx, gy, 1 - gz)
    opposite = (lax.rem(gx + 16, 32), gy, 1 - gz)
    theirs = 9 * gz
    mine = 9 - theirs
    edge = 7 * (1 - gz)
    mid = pl.ds(8, ROWS)
    inner = pl.ds(128, HALF)
    tile = pl.ds(128, WIDE)

    loads = [
        pltpu.make_async_copy(e_hbm, raw.at[0, mid, inner], local_sem.at[0]),
        pltpu.make_async_copy(p_hbm, raw.at[1, mid, inner], local_sem.at[1]),
        pltpu.make_async_copy(seabed_hbm, seabed.at[:, tile], local_sem.at[2]),
        pltpu.make_async_copy(vol_hbm, vol.at[pl.ds(1, LAYERS), mid, tile], local_sem.at[3]),
    ]
    for load in loads:
        load.start()

    barrier = pltpu.get_barrier_semaphore()
    corners = [(-1, -1), (-1, 1), (1, -1), (1, 1)]
    for dx, db in corners + [(-1, 0), (1, 0), (0, -1), (0, 1), (0, -2), (0, 2)]:
        pl.semaphore_signal(barrier, inc=1, device_id=device(dx, db), device_id_type=MESH)
    pl.semaphore_signal(barrier, inc=1, device_id=opposite, device_id_type=MESH)

    lanes = lax.broadcasted_iota(jnp.int32, (ROWS, 128), 1)
    loads[0].wait()
    loads[1].wait()
    e_side, p_side = raw[0, mid, pl.ds(HALF, 128)], raw[1, mid, pl.ds(HALF, 128)]
    side_x[0] = jnp.where(lanes < 8, pltpu.roll(e_side, 8, axis=1), pltpu.roll(p_side, 16, axis=1))
    e_side, p_side = raw[0, mid, pl.ds(128, 128)], raw[1, mid, pl.ds(128, 128)]
    side_x[1] = jnp.where(lanes < 8, e_side, pltpu.roll(p_side, 8, axis=1))
    for d in (0, 1):
        side_send[d, :, pl.ds(0, ROWS)] = jnp.transpose(side_x[d])[:16]

    pl.semaphore_wait(barrier, 11)

    started, made = [], []

    def message(src, dst, to):
        at = len(made)
        assert at < COPIES
        copy = pltpu.make_async_remote_copy(
            src, dst, send_sem.at[at], recv_sem.at[at], device_id=to, device_id_type=MESH
        )
        made.append(copy)
        return copy

    def send(src, dst, to):
        copy = message(src, dst, to)
        copy.start()
        started.append(copy)
        return copy


    row_halos, side_halos = [], []
    for dx, src, dst in ((1, pl.ds(64, 8), pl.ds(0, 8)), (-1, pl.ds(8, 8), pl.ds(72, 8))):
        row_halos.append(send(raw.at[:, src, inner], raw.at[:, dst, inner], device(dx, 0)))
    for d, db in ((0, 1), (1, -1)):
        side_halos.append(send(side_send.at[d], side_recv.at[d], device(0, db)))
        for dx, src, dst in ((1, pl.ds(56, 8), pl.ds(0, 8)), (-1, pl.ds(0, 8), pl.ds(72, 8))):
            row_halos.append(send(side_x.at[d, src], side_in.at[d, dst], device(dx, db)))

    last = pl.ds(DIRECT, ROWS - DIRECT)
    last_in = pl.ds(8 + DIRECT, ROWS - DIRECT)
    hops = [
        message(vol_hbm.at[7, last], relay, opposite),
        message(relay, relay_two, partner),
        message(relay_two, vol.at[0, last_in, tile], opposite),
    ]

    @pl.when(gz == 0)
    def _():
        hops[0].start()

    loads[2].wait()
    loads[3].wait()
    for d, row in ((0, 63), (1, 0)):

        @pl.loop(0, LAYERS)
        def _(k):
            for t in range(16):
                rows_out[d, k, pl.ds(t, 1), :] = vol[
                    k + 1, pl.ds(row + 8, 1), pl.ds(128 + 128 * t, 128)
                ]

        for t in range(16):
            bed = seabed[pl.ds(row, 1), pl.ds(128 + 128 * t, 128)]
            rows_out[d, LAYERS, pl.ds(t, 1), :] = bed.astype(jnp.float32) * DEPTH_UNIT
    row_copies = []
    for d, dx in ((0, 1), (1, -1)):
        row_copies.append(send(rows_out.at[d], rows_in.at[d], device(dx, 0)))
        row_copies.append(send(rows_out.at[d, edge], ring_rows.at[d], device(dx, side)))

    bound_first = send(
        vol_hbm.at[edge, pl.ds(0, FIRST)], vol.at[theirs, pl.ds(8, FIRST), tile], partner
    )
    bound_next = message(
        vol_hbm.at[7, pl.ds(FIRST, DIRECT - FIRST)],
        vol.at[0, pl.ds(8 + FIRST, DIRECT - FIRST), tile],
        partner,
    )
    bound_late = [
        message(
            vol_hbm.at[0, pl.ds(begin, end - begin)],
            vol.at[9, pl.ds(8 + begin, end - begin), tile],
            partner,
        )
        for begin, end in ((FIRST, LATE), (LATE, ROWS))
    ]

    @pl.when(gz == 0)
    def _():
        bound_next.start()

    side_copies = []
    for by, src, dst in (
        (1, pl.ds(WIDE - 128, 128), pl.ds(0, 128)),
        (-1, pl.ds(0, 128), pl.ds(WIDE + 128, 128)),
    ):
        to = device(0, 2 * by)
        side_copies.append(send(vol_hbm.at[:, :, src], vol.at[pl.ds(1, LAYERS), mid, dst], to))
        side_copies.append(send(seabed_hbm.at[:, src], seabed.at[:, dst], to))

    def place_sides(rows):
        for d in (0, 1):
            block_in = side_in[d, rows, :]
            at = pl.ds(0, 128) if d == 0 else pl.ds(HALF + 128, 128)
            raw[0, rows, at] = pltpu.roll(block_in, 120, axis=1) if d == 0 else block_in
            raw[1, rows, at] = pltpu.roll(block_in, 112 if d == 0 else 120, axis=1)

    def tiles(ref, lead, r):
        def rows(i):
            return ref[lead + (pl.ds(pl.multiple_of(8 * i, 8), 8), slice(None))]

        return rows(jnp.maximum(r - 1, 0)), rows(r), rows(jnp.minimum(r + 1, 9))

    def first_section(begin, end):
        @pl.loop(begin, end, unroll=True)
        def _(r):
            height, poten = tiles(raw, (0,), r), tiles(raw, (1,), r)
            rate_height, rate_poten = section(height, poten)
            at = pl.ds(pl.multiple_of(8 * r, 8), 8)
            one[0, at, :] = height[1] + TIME_STEP * rate_height
            one[1, at, :] = poten[1] + TIME_STEP * rate_poten

    def second_section(begin, end):
        @pl.loop(begin, end, unroll=True)
        def _(r):
            height, poten = tiles(one, (0,), r), tiles(one, (1,), r)
            rates = section(height, poten)
            at = pl.ds(pl.multiple_of(8 * r, 8), 8)
            for f in (0, 1):
                first = (height, poten)[f][1]
                new[0, f, at, :] = 0.5 * (raw[f, at, :] + first + TIME_STEP * rates[f])

    def field(f, begin, count):
        rows = pl.ds(begin, count)
        return message(new.at[0, f, rows, inner], new.at[1, f, rows, inner], partner)

    height_copies = [field(0, 24, 32), field(0, 8, 16), field(0, 56, 16)]
    poten_copies = [field(1, 8, 32), field(1, 40, 32)]

    for copy in side_halos:
        copy.wait_recv()
    for d in (0, 1):
        side_in[d, mid, pl.ds(0, 16)] = jnp.transpose(side_recv[d])[:ROWS]
    place_sides(mid)
    first_section(2, 8)

    @pl.when(gz == 1)
    def _():
        hops[0].wait_recv()
        hops[1].start()

    second_section(3, 7)
    height_copies[0].start()
    for copy in row_halos:
        copy.wait_recv()
    place_sides(pl.ds(0, 8))
    place_sides(pl.ds(72, 8))
    first_section(0, 2)
    first_section(8, 10)
    second_section(0, 3)
    height_copies[1].start()
    second_section(7, 10)
    height_copies[2].start()

    for f in (0, 1):
        for d, row in ((0, 7), (1, 72)):
            for t in range(8):
                new_rows_out[f, d, pl.ds(t, 1), :] = new[
                    0, f, pl.ds(row, 1), pl.ds(128 + 128 * t, 128)
                ]
    ring_copies = [send(new_rows_out, new_rows_in, partner)]
    new_e_out[...] = new[0, 0, mid, inner]
    new_p_out[...] = new[0, 1, mid, inner]

    for copy in side_copies:
        copy.wait_recv()
    outer = pl.multiple_of((HALF + 128) * gz, 128)
    left = vol[edge + 1, mid, pl.ds(0, 128)]
    right = vol[edge + 1, mid, pl.ds(WIDE + 128, 128)]
    outer_e = new[0, 0, mid, pl.ds(outer, 128)]
    outer_p = new[0, 1, mid, pl.ds(outer, 128)]

    def pick(x, even, odd):
        return jnp.where(
            gz == 0, pltpu.roll(x, even, axis=1), pltpu.roll(x, odd, axis=1)
        )

    packed = jnp.where(
        lanes < 2,
        jnp.where(lanes == 0, pltpu.roll(left, 1, axis=1), pltpu.roll(right, 1, axis=1)),
        jnp.where(lanes == 2, pick(outer_e, 3, 2), pick(outer_p, 4, 3)),
    )
    cols_out[:, pl.ds(0, ROWS)] = jnp.transpose(packed)[:8]
    ring_copies.append(send(cols_out, cols_in, partner))

    @pl.loop(0, 8)
    def _(r):
        at = pl.multiple_of(8 * r, 8)
        depth[pl.ds(at + 8, 8), :] = seabed[pl.ds(at, 8), :].astype(jnp.float32) * DEPTH_UNIT

    def start_of(h):
        return HALF * (gz if h == 0 else 1 - gz)

    def around(ref, lead, row, lane):
        def rows(at, lanes):
            return ref[lead + (pl.ds(at, 8), lanes)]

        wide = rows(row, pl.ds(lane, HALF + 256))
        here = wide[:, 128 : 128 + HALF]
        centre = pl.ds(pl.multiple_of(lane + 128, 128), HALF)
        before, after = rows(row - 8, centre), rows(row + 8, centre)
        up, down = row_shift(before, here, after, 1), row_shift(before, here, after, -1)
        right = lane_shift(wide, 1)[:, 128 : 128 + HALF]
        left = lane_shift(wide, -1)[:, 128 : 128 + HALF]
        return here, up - down, right - left, (up + down) + (right + left)

    def difference(layer, r, lane, flat):
        row = pl.multiple_of(8 * r, 8)
        here, by_row, by_lane, total = around(vol, (layer,), pl.multiple_of(row + 8, 8), lane)
        at = (pl.ds(row, 8), pl.ds(lane, HALF))
        north[(layer,) + at] = by_row
        east[(layer,) + at] = by_lane
        if flat:
            lap_ref[(layer - 1,) + at] = total - 4.0 * here

    def differences(layer, h, first_tile, last_tile, flat):
        lane = pl.multiple_of(start_of(h), 128)

        @pl.loop(first_tile, last_tile, unroll=True)
        def _(r):
            difference(layer, r, lane, flat)

    def coefficients(h):
        lane = pl.multiple_of(start_of(h), 128)
        span = pl.ds(lane, HALF + 256)

        @pl.loop(0, 10, unroll=2)
        def _(r):
            at = pl.ds(pl.multiple_of(8 * r, 8), 8)
            column[h, at, :] = depth[at, span] + new[h, 0, at, :]

        @pl.loop(0, 8, unroll=4)
        def _(r):
            row = pl.multiple_of(8 * r, 8)
            inside = pl.multiple_of(row + 8, 8)
            here, column_north, column_east, _ = around(column, (h,), inside, 0)
            _, depth_north, depth_east, _ = around(depth, (), inside, lane)
            inverse = 1.0 / here
            scale = 4.0 * inverse
            at = (pl.ds(row, 8), pl.ds(lane, HALF))
            coef[(0,) + at] = depth_north * scale
            coef[(1,) + at] = column_north * scale
            coef[(2,) + at] = depth_east * scale
            coef[(3,) + at] = column_east * scale
            coef[(4,) + at] = 64.0 * inverse * inverse

    def top(h, begin, end):
        span = pl.ds(pl.multiple_of(start_of(h), 128), HALF + 256)

        @pl.loop(begin, end)
        def _(r):
            at = pl.ds(pl.multiple_of(8 * r, 8), 8)
            vol[9, at, span] = 2.0 * new[h, 1, at, :] - vol[8, at, span]

    def combine(h, start, count, first_tile, last_tile):
        base = start_of(h)
        sigma = (jnp.asarray(8 * gz + start, jnp.int32).astype(jnp.float32) + 0.5) * 0.0625
        lowest = jnp.where(start + gz == 0, 1, start)

        strip = HALF if count == 1 else STRIP

        @pl.loop(first_tile, last_tile, unroll=count == 1)
        def _(r):
            rows = pl.ds(pl.multiple_of(8 * r, 8), 8)
            inside = pl.ds(pl.multiple_of(8 * r + 8, 8), 8)

            @pl.loop(0, HALF // strip)
            def _(s):
                lane = base + s * strip
                at = (rows, pl.ds(pl.multiple_of(lane, 128), strip))
                centre = (inside, pl.ds(pl.multiple_of(lane + 128, 128), strip))

                def load(layer):
                    return (
                        vol[(layer,) + centre], north[(layer,) + at], east[(layer,) + at]
                    )

                step_north, step_east = coef[(1,) + at], coef[(3,) + at]
                slope_north = coef[(0,) + at] - sigma * step_north
                slope_east = coef[(2,) + at] - sigma * step_east
                step_north = step_north * 0.0625
                step_east = step_east * 0.0625
                bottom = coef[(4,) + at]
                below, middle = load(lowest), load(start + 1)
                for k in range(count):
                    above = load(start + k + 2)
                    weight = slope_north * slope_north + slope_east * slope_east + bottom
                    vertical = 4.0 * (above[0] + below[0]) - 8.0 * middle[0]
                    lap_ref[(start + k,) + at] = (
                        lap_ref[(start + k,) + at]
                        + slope_north * (above[1] - below[1])
                        + slope_east * (above[2] - below[2])
                        + weight * vertical
                    )
                    if k < count - 1:
                        slope_north = slope_north - step_north
                        slope_east = slope_east - step_east
                    below, middle = middle, above

    def all_layers(begin, end, step):
        @pl.loop(begin, end, step=step)
        def _(r):
            @pl.loop(0, 2)
            def _(s):
                for layer in range(1, LAYERS + 1):
                    difference(layer, r, pl.multiple_of(HALF * s, 128), True)

    all_layers(1, 7, 1)

    @pl.when(gz == 0)
    def _():
        for copy in poten_copies:
            copy.start()
        hops[1].wait_recv()
        hops[2].start()

    @pl.when(gz == 1)
    def _():
        for copy in bound_late:
            copy.start()

    for copy in row_copies:
        copy.wait_recv()
    for d, row in ((0, 7), (1, 72)):

        @pl.loop(0, LAYERS)
        def _(k):
            for t in range(16):
                vol[k + 1, pl.ds(row, 1), pl.ds(128 + 128 * t, 128)] = rows_in[d, k, pl.ds(t, 1), :]

        for t in range(16):
            at = pl.ds(128 + 128 * t, 128)
            depth[pl.ds(row, 1), at] = rows_in[d, LAYERS, pl.ds(t, 1), :]

    all_layers(0, 8, 7)

    @pl.when(gz == 1)
    def _():
        top(0, 0, 10)
        differences(9, 0, 0, 8, False)

    coefficients(0)
    combine(0, gz, LAYERS - 1, 0, 8)

    for copy in ring_copies:
        copy.wait_recv()
    for d, row in ((0, 7), (1, 72)):
        for t in range(16):
            vol[mine, pl.ds(row, 1), pl.ds(128 + 128 * t, 128)] = ring_rows[d, pl.ds(t, 1), :]
        for f in (0, 1):
            for t in range(8):
                new[1, f, pl.ds(row, 1), pl.ds(128 + 128 * t, 128)] = new_rows_in[
                    f, d, pl.ds(t, 1), :
                ]
    back = jnp.transpose(cols_in[...])[:ROWS]
    back = jnp.concatenate([back, jnp.zeros((ROWS, 128 - 8), jnp.float32)], axis=1)
    vol[mine, mid, pl.ds(0, 128)] = pltpu.roll(back, 127, axis=1)
    vol[mine, mid, pl.ds(WIDE + 128, 128)] = pltpu.roll(back, 127, axis=1)
    far = pl.multiple_of((HALF + 128) * (1 - gz), 128)
    close = pl.multiple_of((HALF + 128) * gz, 128)
    inside = pl.multiple_of(HALF * (1 - gz) + 128 * gz, 128)
    for f in (0, 1):
        new[1, f, mid, pl.ds(far, 128)] = pick(back, 126 - f, 125 - f)
        new[1, f, mid, pl.ds(close, 128)] = new[0, f, mid, pl.ds(inside, 128)]

    bound_first.wait_recv()

    @pl.when(gz == 1)
    def _():
        bound_next.wait_recv()

    def other_half():
        for copy in height_copies:
            copy.wait_recv()
        coefficients(1)

    @pl.when(gz == 0)
    def _():
        split = FIRST // 8 - 1
        for h in (0, 1):
            differences(9, h, 0, split, False)
        combine(0, LAYERS - 1, 1, 0, split)
        other_half()
        combine(1, 0, LAYERS - 1, 0, 8)
        combine(1, LAYERS - 1, 1, 0, split)
        for copy, first, last in zip(bound_late, (split, LATE // 8 - 1), (LATE // 8 - 1, 8)):
            copy.wait_recv()
            for h in (0, 1):
                differences(9, h, first, last, False)
                combine(h, LAYERS - 1, 1, first, last)

    @pl.when(gz == 1)
    def _():
        split = DIRECT // 8 - 1
        for h in (0, 1):
            differences(0, h, 0, split, False)
        combine(0, 0, 1, 0, split)
        other_half()
        combine(1, 1, LAYERS - 2, 0, 8)
        combine(1, 0, 1, 0, split)
        hops[2].wait_recv()
        for h in (0, 1):
            differences(0, h, split, 8, False)
            combine(h, 0, 1, split, 8)
        for copy, (begin, end), (first, last) in zip(
            poten_copies, ((0, 5), (5, 10)), ((0, 3), (3, 8))
        ):
            copy.wait_recv()
            top(1, begin, end)
            differences(9, 1, first, last, False)
            combine(1, LAYERS - 1, 1, first, last)

    for copy in height_copies:
        copy.wait_send()

    @pl.when(gz == 0)
    def _():
        for copy in (*poten_copies, bound_next, hops[0], hops[2]):
            copy.wait_send()

    @pl.when(gz == 1)
    def _():
        for copy in (hops[1], *bound_late):
            copy.wait_send()

    for copy in started:
        copy.wait_send()


def write(e_ref, p_ref, lap_ref, e_out, p_out, lap_out, sem):
    pairs = [(lap_ref.at[k], lap_out.at[k]) for k in range(LAYERS)]
    pairs += [(e_ref, e_out), (p_ref, p_out)]
    copies = [pltpu.make_async_copy(*pair, sem.at[i]) for i, pair in enumerate(pairs)]
    for copy in copies:
        copy.start()
    for copy in copies:
        copy.wait()


def shards(elevation, surface_potential, seabed, interior_potential):
    hbm = pl.BlockSpec(memory_space=pltpu.HBM)
    vmem = pl.BlockSpec(memory_space=pltpu.VMEM)
    f32 = jnp.float32
    held = (
        pltpu.VMEM((ROWS, HALF), f32),
        pltpu.VMEM((ROWS, HALF), f32),
        pltpu.VMEM((LAYERS, ROWS, WIDE), f32),
    )
    operands = [
        pltpu.with_memory_space_constraint(x, pltpu.HBM)
        for x in (elevation, surface_potential, seabed, interior_potential)
    ]
    results = pl.pallas_call(
        kernel,
        out_shape=held,
        in_specs=[hbm] * 4,
        out_specs=(vmem,) * 3,
        scratch_shapes=[
            pltpu.VMEM((2, ROWS + 16, HALF + 256), f32),
            pltpu.VMEM((2, ROWS + 16, HALF + 256), f32),
            pltpu.VMEM((2, 2, ROWS + 16, HALF + 256), f32),
            pltpu.VMEM((ROWS, WIDE + 256), jnp.int32),
            pltpu.VMEM((LAYERS + 2, ROWS + 16, WIDE + 256), f32),
            pltpu.VMEM((ROWS + 16, WIDE + 256), f32),
            pltpu.VMEM((2, ROWS + 16, HALF + 256), f32),
            pltpu.VMEM((LAYERS + 2, ROWS, WIDE), f32),
            pltpu.VMEM((LAYERS + 2, ROWS, WIDE), f32),
            pltpu.VMEM((5, ROWS, WIDE), f32),
            pltpu.VMEM((2, ROWS, 128), f32),
            pltpu.VMEM((2, 16, 128), f32),
            pltpu.VMEM((2, 16, 128), f32),
            pltpu.VMEM((2, ROWS + 16, 128), f32),
            pltpu.VMEM((ROWS - DIRECT, WIDE), f32),
            pltpu.VMEM((ROWS - DIRECT, WIDE), f32),
            pltpu.VMEM((2, LAYERS + 1, 16, 128), f32),
            pltpu.VMEM((2, LAYERS + 1, 16, 128), f32),
            pltpu.VMEM((2, 16, 128), f32),
            pltpu.VMEM((2, 2, 8, 128), f32),
            pltpu.VMEM((2, 2, 8, 128), f32),
            pltpu.VMEM((8, 128), f32),
            pltpu.VMEM((8, 128), f32),
            pltpu.SemaphoreType.DMA((4,)),
            pltpu.SemaphoreType.DMA((COPIES,)),
            pltpu.SemaphoreType.DMA((COPIES,)),
        ],
        compiler_params=pltpu.CompilerParams(
            collective_id=0, has_side_effects=True, vmem_limit_bytes=48 << 20
        ),
        name="wave_step",
    )(*operands)
    return pl.pallas_call(
        write,
        out_shape=tuple(jax.ShapeDtypeStruct(x.shape, f32) for x in results),
        in_specs=[vmem] * 3,
        out_specs=(hbm,) * 3,
        scratch_shapes=[pltpu.SemaphoreType.DMA((LAYERS + 2,))],
        compiler_params=pltpu.CompilerParams(vmem_limit_bytes=4 << 20),
        name="write_results",
    )(*(pltpu.with_memory_space_constraint(x, pltpu.VMEM) for x in results))


def solution(mesh):
    return jax.shard_map(
        shards,
        mesh=mesh,
        in_specs=(P("gx", ("gy", "gz")), P("gx", ("gy", "gz")), P("gx", "gy"), P("gz", "gx", "gy")),
        out_specs=(P("gx", ("gy", "gz")), P("gx", ("gy", "gz")), P("gz", "gx", "gy")),
        check_vma=False,
    )
```
